32 devices in a mesh: dp: 8 (over z, x), row: 2 (over y), col: 2 (over core).
Axes of the slice: x: 2, y: 2, z: 4, core: 2. Of those that a mesh axis runs over, the one named last changes fastest.
Arguments:
- layer_input: bfloat16 [16384, 768], P(('dp', 'row', 'col')), may hold values from -14 to 14
- encoder_states: bfloat16 [16384, 768], P(('dp', 'row', 'col')), may hold values from -6 to 6
- cotangent: float32 [16384, 768], P(('dp', 'row', 'col')), may hold values from -6 to 6
- buckets: int32 [512], replicated, may hold values from 0 to 31, never falling along the last dimension, each value on 1 to 128 neighbouring positions
- gain_self: float32 [768], P(('row', 'col')), may hold values from 0.5 to 1.5
- gain_cross: float32 [768], P(('row', 'col')), may hold values from 0.5 to 1.5
- gain_ffn: float32 [768], P(('row', 'col')), may hold values from 0.5 to 1.5
- self_query: bfloat16 [768, 768], P('row', 'col'), may hold values from -0.0546875 to 0.0546875
- self_key: bfloat16 [768, 768], P('row', 'col'), may hold values from -0.21875 to 0.21875
- self_value: bfloat16 [768, 768], P('row', 'col'), may hold values from -0.21875 to 0.21875
- self_out: bfloat16 [768, 768], P('col', 'row'), may hold values from -0.625 to 0.625
- cross_query: bfloat16 [768, 768], P('row', 'col'), may hold values from -0.0546875 to 0.0546875
- cross_key: bfloat16 [768, 768], P('row', 'col'), may hold values from -0.21875 to 0.21875
- cross_value: bfloat16 [768, 768], P('row', 'col'), may hold values from -0.21875 to 0.21875
- cross_out: bfloat16 [768, 768], P('col', 'row'), may hold values from -0.625 to 0.625
- ffn_gate: bfloat16 [768, 2048], P('row', 'col'), may hold values from -0.21875 to 0.21875
- ffn_up: bfloat16 [768, 2048], P('row', 'col'), may hold values from -0.21875 to 0.21875
- ffn_down: bfloat16 [2048, 768], P('col', 'row'), may hold values from -0.125 to 0.125
- rel_table: float32 [2, 2, 3, 32], P('col', 'row'), may hold values from -4 to 4
Outputs:
- layer_output: float32 [16384, 768], P(('dp', 'row', 'col'))
- input_grad: float32 [16384, 768], P(('dp', 'row', 'col'))
- encoder_grad: float32 [16384, 768], P(('dp', 'row', 'col'))
- gain_self_grad: float32 [768], P(('row', 'col'))
- gain_cross_grad: float32 [768], P(('row', 'col'))
- gain_ffn_grad: float32 [768], P(('row', 'col'))
- self_query_grad: float32 [768, 768], P('row', 'col')
- self_key_grad: float32 [768, 768], P('row', 'col')
- self_value_grad: float32 [768, 768], P('row', 'col')
- self_out_grad: float32 [768, 768], P('col', 'row')
- cross_query_grad: float32 [768, 768], P('row', 'col')
- cross_key_grad: float32 [768, 768], P('row', 'col')
- cross_value_grad: float32 [768, 768], P('row', 'col')
- cross_out_grad: float32 [768, 768], P('col', 'row')
- ffn_gate_grad: float32 [768, 2048], P('row', 'col')
- ffn_up_grad: float32 [768, 2048], P('row', 'col')
- ffn_down_grad: float32 [2048, 768], P('col', 'row')
- table_grad: float32 [2, 2, 3, 32], P('col', 'row')
The draws below stay inside these ranges and needn't reach their ends.
Inputs may be any that keep to these rules, and one draw needn't show every extreme that they name: buckets never falls as the distance grows, and each of the 32 buckets is the bucket of some distance.
All inputs are finite; a program needn't handle non-finite values.
Results may differ from the reference program's by a relative error of at most 0.028.
Values may be sent and summed in bfloat16 or wider, within the bound.
No kernel may reach another device: no remote copies, remote signals or barrier semaphores. Data moves between devices by JAX's collectives and lax.ppermute only.
A program may use at most 256 MiB of HBM per device.

```python
import math
import jax
import jax.numpy as jnp
import numpy as np
from jax import lax

D = 768
H = 12
HD = 64
FF = 2048
NB = 32
LEN = 512
ENC_LEN = 512
HEAD_DEV = 3
TOKENS = 16384
ENC_TOKENS = 16384
N_ROW = 2
N_COL = 2


def draw_layer_input(key, part):
    bulk_key, pick_key, sign_key, strength_key = jax.random.split(key, 4)
    feature_count = max(2, D // 96)
    order = jax.random.permutation(pick_key, D)
    chosen = (order < feature_count).astype(jnp.float32)
    signs = jax.random.randint(sign_key, (D,), 0, 2).astype(jnp.float32) * 2.0 - 1.0
    bulk = jnp.clip(jax.random.normal(bulk_key, (TOKENS, D), jnp.float32), -6.0, 6.0)
    strength = jax.random.uniform(strength_key, (TOKENS, 1), jnp.float32, 3.0, 7.0)
    values = bulk + strength * (chosen * signs)[None, :]
    return values.astype(jnp.bfloat16)


def block_levels(key, shape, pieces, smallest, high):
    factor_of = 1.0
    for position, parts in pieces:
        heights = jax.random.uniform(jax.random.fold_in(jax.random.fold_in(key, 6), position), (parts,), jnp.float32, smallest / len(pieces), high / len(pieces))
        factor_of = factor_of * jnp.repeat(jnp.exp(heights), shape[position] // parts).reshape((-1,) + (1,) * (len(shape) - 1 - position))
    return factor_of


def length_profile(count, total, limit, slope):
    weights = [(1 << 20) // math.isqrt(standing ** slope) + 1 for standing in range(2, count + 1)]
    rest, holding = total - limit - (count - 1), [1] * (count - 1)
    while rest > 0:
        movable = [i for i in range(count - 1) if holding[i] < limit]
        whole, budget = sum([weights[i] for i in movable]), rest
        for i in movable:
            addition = min(limit - holding[i], max(1, budget * weights[i] // whole), rest)
            holding[i] = holding[i] + addition
            rest = rest - addition
    return np.array([limit] + holding)


def uneven_parts(rng, amount, total, reach, slope):
    if amount == 2:
        one = jax.random.randint(rng, (), max(1, total - reach), min(reach, total - 1) + 1)
        return jnp.stack([one, total - one])
    tallies = jnp.asarray(length_profile(amount, total, reach, slope), jnp.int32)
    pairs = (amount - 1) // 2
    donor, receiver = tallies[1:1 + 2 * pairs:2], tallies[2:2 + 2 * pairs:2]
    margin = jnp.minimum(donor - 1, reach - receiver)
    shifted = jax.random.randint(jax.random.fold_in(rng, 1), (pairs,), 0, 1 << 20) % (margin + 1)
    tallies = tallies.at[1:1 + 2 * pairs:2].set(donor - shifted).at[2:2 + 2 * pairs:2].set(receiver + shifted)
    return tallies[jax.random.permutation(jax.random.fold_in(rng, 2), amount)]


def centred(own_key, dims, scale, limit, cuts=(), kind=jnp.bfloat16):
    array = scale * jax.random.normal(own_key, dims, jnp.float32)
    if cuts:
        array = array * block_levels(own_key, dims, cuts, -0.22, 0.18)
    return jnp.clip(array, -limit, limit).astype(kind)


def setup_inputs(seed: int = 0) -> dict:
    streams_of = jax.random.split(jax.random.key(seed), 20)
    return {
        "layer_input": draw_layer_input(jax.random.fold_in(streams_of[19], 71), 0),
        "encoder_states": centred(streams_of[1], (ENC_TOKENS, D), 1.0, 6.0, ((0, 32),)),
        "cotangent": centred(streams_of[2], (TOKENS, D), 1.0, 6.0, ((0, 32),), jnp.float32),
        "buckets": jnp.searchsorted(jnp.cumsum(uneven_parts(streams_of[3], NB, LEN, LEN // 4, 2)), jnp.arange(LEN), side="right").astype(jnp.int32),
        "gain_self": jnp.clip(1.0 + 0.1 * jax.random.normal(streams_of[4], (D,), jnp.float32), 0.5, 1.5),
        "gain_cross": jnp.clip(1.0 + 0.1 * jax.random.normal(streams_of[5], (D,), jnp.float32), 0.5, 1.5),
        "gain_ffn": jnp.clip(1.0 + 0.1 * jax.random.normal(streams_of[6], (D,), jnp.float32), 0.5, 1.5),
        "self_query": centred(streams_of[7], (D, H * HD), (16 * D) ** -0.5, 0.0546875, ((0, 2), (1, 2))),
        "self_key": centred(streams_of[8], (D, H * HD), D ** -0.5, 0.21875, ((0, 2), (1, 2))),
        "self_value": centred(streams_of[9], (D, H * HD), D ** -0.5, 0.21875, ((0, 2), (1, 2))),
        "self_out": centred(streams_of[10], (H * HD, D), (H * HD // 8) ** -0.5, 0.625, ((0, 2), (1, 2))),
        "cross_query": centred(streams_of[11], (D, H * HD), (16 * D) ** -0.5, 0.0546875, ((0, 2), (1, 2))),
        "cross_key": centred(streams_of[12], (D, H * HD), D ** -0.5, 0.21875, ((0, 2), (1, 2))),
        "cross_value": centred(streams_of[13], (D, H * HD), D ** -0.5, 0.21875, ((0, 2), (1, 2))),
        "cross_out": centred(streams_of[14], (H * HD, D), (H * HD // 8) ** -0.5, 0.625, ((0, 2), (1, 2))),
        "ffn_gate": centred(streams_of[15], (D, FF), D ** -0.5, 0.21875, ((0, 2), (1, 2))),
        "ffn_up": centred(streams_of[16], (D, FF), D ** -0.5, 0.21875, ((0, 2), (1, 2))),
        "ffn_down": centred(streams_of[17], (FF, D), FF ** -0.5, 0.125, ((0, 2), (1, 2))),
        "rel_table": centred(streams_of[18], (N_COL, N_ROW, HEAD_DEV, NB), 1.0, 4.0, ((0, 2), (1, 2)), jnp.float32),
    }


epsilon = 1e-06
masked_score = -1e+30

@jax.custom_vjp
def low(v):
    return lax.optimization_barrier(v.astype(jnp.bfloat16)).astype(jnp.float32)

@jax.custom_vjp
def low_back(v):
    return v

def low_keep(v):
    return (low(v), None)

def low_pass(kept, grad):
    return (grad,)

def back_keep(v):
    return (v, None)

def back_low(kept, grad):
    return (low(grad),)
low.defvjp(low_keep, low_pass)
low_back.defvjp(back_keep, back_low)

def matmul(left_side, right_side):
    return jnp.dot(left_side, right_side, precision=lax.Precision.HIGHEST, preferred_element_type=jnp.float32)

def rms_norm(values, gain_values):
    rescale = lax.rsqrt(lax.optimization_barrier(jnp.mean(values * values, axis=-1, keepdims=True)) + epsilon)
    return values * rescale * gain_values

def rounded_both(values):
    return low_back(low(values))

def attend(queries, key_rows, value_rows, rel_bias, causal):
    scores = jnp.einsum('qhd,khd->hqk', queries, key_rows, precision=lax.Precision.HIGHEST)
    if rel_bias is not None:
        scores = scores + rel_bias
    scores = low_back(scores)
    if causal is not None:
        scores = jnp.where(causal[None, :, :], scores, masked_score)
    weights = low(jax.nn.softmax(scores, axis=-1))
    return jnp.einsum('hqk,khd->qhd', weights, value_rows, precision=lax.Precision.HIGHEST)

def make_layer(buckets):

    def forward(layer_input, encoder_states, gain_self, gain_cross, gain_ffn, self_query, self_key, self_value, self_out, cross_query, cross_key, cross_value, cross_out, ffn_gate, ffn_up, ffn_down, rel_table):
        token_count = layer_input.shape[0]
        sequences = token_count // LEN
        positions = jnp.arange(LEN, dtype=jnp.int32)
        onehot = (buckets[:, None] == jnp.arange(NB, dtype=jnp.int32)[None, :]).astype(jnp.float32)
        by_distance = matmul(rel_table.reshape(H, NB), onehot.T)
        distance = jnp.clip(positions[:, None] - positions[None, :], 0, LEN - 1).astype(jnp.int32)
        rel_bias = jnp.take(by_distance, distance, axis=1)
        causal = positions[:, None] >= positions[None, :]

        def split_heads(values, length):
            return values.reshape(sequences, length, H, HD)

        def self_sequence(operands):
            return attend(operands[0], operands[1], operands[2], rel_bias, causal)

        def cross_sequence(operands):
            return attend(operands[0], operands[1], operands[2], None, None)
        normed = low(rms_norm(layer_input, gain_self))
        queries = rounded_both(matmul(normed, self_query))
        key_rows = rounded_both(matmul(normed, self_key))
        value_rows = rounded_both(matmul(normed, self_value))
        attended = lax.map(jax.checkpoint(self_sequence), (split_heads(queries, LEN), split_heads(key_rows, LEN), split_heads(value_rows, LEN)))
        attended = rounded_both(attended.reshape(token_count, H * HD))
        middle = layer_input + low_back(matmul(attended, self_out))
        normed = low(rms_norm(middle, gain_cross))
        cross_queries = rounded_both(matmul(normed, cross_query))
        cross_keys = rounded_both(matmul(encoder_states, cross_key))
        cross_values = rounded_both(matmul(encoder_states, cross_value))
        mixture = lax.map(jax.checkpoint(cross_sequence), (split_heads(cross_queries, LEN), split_heads(cross_keys, ENC_LEN), split_heads(cross_values, ENC_LEN)))
        mixture = rounded_both(mixture.reshape(token_count, H * HD))
        after_cross = middle + low_back(matmul(mixture, cross_out))
        normed = low(rms_norm(after_cross, gain_ffn))
        gate_value = low_back(matmul(normed, ffn_gate))
        up_value = low_back(matmul(normed, ffn_up))
        hidden = low(jax.nn.gelu(gate_value, approximate=True) * up_value)
        return after_cross + low_back(matmul(hidden, ffn_down))
    return forward

def reference(layer_input, encoder_states, cotangent, buckets, gain_self, gain_cross, gain_ffn, self_query, self_key, self_value, self_out, cross_query, cross_key, cross_value, cross_out, ffn_gate, ffn_up, ffn_down, rel_table):
    forward = make_layer(buckets)
    floats = (layer_input.astype(jnp.float32), encoder_states.astype(jnp.float32), gain_self.astype(jnp.float32), gain_cross.astype(jnp.float32), gain_ffn.astype(jnp.float32), self_query.astype(jnp.float32), self_key.astype(jnp.float32), self_value.astype(jnp.float32), self_out.astype(jnp.float32), cross_query.astype(jnp.float32), cross_key.astype(jnp.float32), cross_value.astype(jnp.float32), cross_out.astype(jnp.float32), ffn_gate.astype(jnp.float32), ffn_up.astype(jnp.float32), ffn_down.astype(jnp.float32), rel_table.astype(jnp.float32))
    result, layer_back = jax.vjp(forward, *floats)
    gradients = layer_back(cotangent.astype(jnp.float32))
    return (result, gradients[0], gradients[1], gradients[2], gradients[3], gradients[4], gradients[5], gradients[6], gradients[7], gradients[8], gradients[9], gradients[10], gradients[11], gradients[12], gradients[13], gradients[14], gradients[15], gradients[16])
```

```python
import functools

import jax
import jax.numpy as jnp
from jax import lax
from jax.experimental import pallas as pl
from jax.experimental.pallas import tpu as pltpu
from jax.sharding import PartitionSpec as P

D = 768
HD = 64
NB = 32
LEN = 512
BLK = 128
HALF = D // 2
PAIRS = HALF // (2 * HD)

epsilon = 1e-06
masked_score = -1e30
f32 = jnp.float32
bf16 = jnp.bfloat16
SWAP = [(0, 1), (1, 0)]


def over_row(x):
    return lax.ppermute(x, "row", SWAP)


def over_col(x):
    return lax.ppermute(x, "col", SWAP)


def dot(a, b):
    return jnp.dot(a, b, preferred_element_type=f32)


def dot_t(a, b):
    return lax.dot_general(a, b, (((1,), (1,)), ((), ())), preferred_element_type=f32)


def t_dot(a, b):
    return lax.dot_general(a, b, (((0,), (0,)), ((), ())), preferred_element_type=f32)


def local_order(x, flag, axis):
    first, second = jnp.split(x, 2, axis=axis)
    swapped = jnp.concatenate([second, first], axis=axis)
    return jnp.where(flag == 0, x, swapped)


def causal_mask():
    rows = lax.broadcasted_iota(jnp.int32, (BLK, BLK), 0)
    cols = lax.broadcasted_iota(jnp.int32, (BLK, BLK), 1)
    return rows >= cols


def softmax_rows(scores):
    top = jnp.max(scores, axis=1, keepdims=True)
    shifted = jnp.exp(scores - top)
    total = jnp.sum(shifted, axis=1, keepdims=True)
    return (shifted * (1.0 / total)).astype(bf16)


def self_fwd_kernel(q_ref, k_ref, v_ref, bias_ref, out_ref, probs_ref):
    mask = causal_mask()
    for head in range(2):
        lanes = slice(head * HD, (head + 1) * HD)
        row = jnp.broadcast_to(bias_ref[0, head : head + 1, :], (BLK, LEN))
        bias = pltpu.roll(row, 0, 1, stride=1, stride_axis=0)
        for block in range(LEN // BLK):
            rows = slice(block * BLK, (block + 1) * BLK)
            wide = (block + 1) * BLK
            scores = dot_t(q_ref[rows, lanes], k_ref[:wide, lanes])
            scores = scores + bias[:, LEN - wide :]
            last = jnp.where(mask, scores[:, wide - BLK :], masked_score)
            if block:
                scores = jnp.concatenate([scores[:, : wide - BLK], last], axis=1)
            else:
                scores = last
            probs = softmax_rows(scores)
            probs_ref[head, rows, :wide] = probs
            out_ref[rows, lanes] = dot(probs, v_ref[:wide, lanes]).astype(bf16)


def cross_fwd_kernel(q_ref, k_ref, v_ref, out_ref, probs_ref):
    for head in range(2):
        lanes = slice(head * HD, (head + 1) * HD)
        for block in range(LEN // BLK):
            rows = slice(block * BLK, (block + 1) * BLK)
            scores = dot_t(q_ref[rows, lanes], k_ref[:, lanes])
            probs = softmax_rows(scores)
            probs_ref[head, rows, :] = probs
            out_ref[rows, lanes] = dot(probs, v_ref[:, lanes]).astype(bf16)


def score_grad_of(probs, weight_grads):
    wide = probs.astype(f32)
    mixed = wide * weight_grads
    inner = jnp.sum(mixed, axis=1, keepdims=True)
    return mixed - wide * inner


def shift_sum(total):
    acc = total[:8]
    for first in range(8, BLK, 8):
        acc = acc + pltpu.roll(total[first : first + 8], LEN - first, 1)
    line = lax.broadcasted_iota(jnp.int32, (8, LEN), 0)
    for bit in (1, 2, 4):
        acc = jnp.where((line & bit) != 0, pltpu.roll(acc, LEN - bit, 1), acc)
    return jnp.sum(acc, axis=0, keepdims=True)


def self_bwd_kernel(q_ref, k_ref, v_ref, g_ref, probs_ref, dq_ref, dk_ref, dv_ref, shift_ref, ds_ref):
    for head in range(2):
        lanes = slice(head * HD, (head + 1) * HD)
        total = jnp.zeros((BLK, LEN), f32)
        for block in range(LEN // BLK):
            rows = slice(block * BLK, (block + 1) * BLK)
            wide = (block + 1) * BLK
            weight_grads = dot_t(g_ref[rows, lanes], v_ref[:wide, lanes])
            grads = score_grad_of(probs_ref[head, rows, :wide], weight_grads)
            if wide < LEN:
                total = total + jnp.concatenate([jnp.zeros((BLK, LEN - wide), f32), grads], axis=1)
            else:
                total = total + grads
            short = grads.astype(bf16)
            ds_ref[rows, :wide] = short
            dq_ref[rows, lanes] = dot(short, k_ref[:wide, lanes]).astype(bf16)
        for block in range(LEN // BLK):
            cols = slice(block * BLK, (block + 1) * BLK)
            rest = slice(block * BLK, LEN)
            dk_ref[cols, lanes] = t_dot(ds_ref[rest, cols], q_ref[rest, lanes]).astype(bf16)
            dv_ref[cols, lanes] = t_dot(probs_ref[head, rest, cols], g_ref[rest, lanes]).astype(bf16)
        shift_ref[0, head : head + 1, :] = shift_sum(total)


def cross_bwd_kernel(q_ref, k_ref, v_ref, g_ref, probs_ref, dq_ref, dk_ref, dv_ref, ds_ref):
    for head in range(2):
        lanes = slice(head * HD, (head + 1) * HD)
        for block in range(LEN // BLK):
            rows = slice(block * BLK, (block + 1) * BLK)
            weight_grads = dot_t(g_ref[rows, lanes], v_ref[:, lanes])
            short = score_grad_of(probs_ref[head, rows, :], weight_grads).astype(bf16)
            ds_ref[rows, :] = short
            dq_ref[rows, lanes] = dot(short, k_ref[:, lanes]).astype(bf16)
        dk_ref[:, lanes] = t_dot(ds_ref[...], q_ref[:, lanes]).astype(bf16)
        dv_ref[:, lanes] = t_dot(probs_ref[head], g_ref[:, lanes]).astype(bf16)


def lane_block(first):
    return pl.BlockSpec((LEN, 2 * HD), lambda s, g: (s, first + g))


PROBS = pl.BlockSpec((2, LEN, LEN), lambda s, g: (s * PAIRS + g, 0, 0))
BIAS = pl.BlockSpec((1, 2, LEN), lambda s, g: (g, 0, 0))
SHIFT = pl.BlockSpec((1, 2, LEN), lambda s, g: (s * PAIRS + g, 0, 0))


def cost(flops, moved):
    return pl.CostEstimate(flops=flops, bytes_accessed=moved, transcendentals=0)


def attention_fwd(queries, query_at, keys, key_at, values, value_at, bias):
    tokens = queries.shape[0]
    sequences = tokens // LEN
    specs = [lane_block(query_at), lane_block(key_at), lane_block(value_at)]
    operands = [queries, keys, values]
    if bias is not None:
        specs.append(BIAS)
        operands.append(bias)
    return pl.pallas_call(
        cross_fwd_kernel if bias is None else self_fwd_kernel,
        grid=(sequences, PAIRS),
        in_specs=specs,
        out_specs=[lane_block(0), PROBS],
        out_shape=[
            jax.ShapeDtypeStruct((tokens, HALF), bf16),
            jax.ShapeDtypeStruct((sequences * PAIRS * 2, LEN, LEN), bf16),
        ],
        cost_estimate=cost(4 * tokens * LEN * HALF * 4, tokens * LEN * 12),
    )(*operands)


def attention_bwd(queries, query_at, keys, key_at, values, value_at, grads, probs, causal):
    tokens = queries.shape[0]
    sequences = tokens // LEN
    piece = jax.ShapeDtypeStruct((tokens, HALF), bf16)
    out_shape = [piece] * 3
    out_specs = [lane_block(0)] * 3
    if causal:
        out_shape.append(jax.ShapeDtypeStruct((sequences * PAIRS, 2, LEN), f32))
        out_specs.append(SHIFT)
    return pl.pallas_call(
        self_bwd_kernel if causal else cross_bwd_kernel,
        grid=(sequences, PAIRS),
        in_specs=[lane_block(query_at), lane_block(key_at), lane_block(value_at), lane_block(0), PROBS],
        out_specs=out_specs,
        out_shape=out_shape,
        scratch_shapes=[pltpu.VMEM((LEN, LEN), bf16)],
        cost_estimate=cost(8 * tokens * LEN * HALF * 4, tokens * LEN * 12),
    )(queries, keys, values, grads, probs)


def normalize(values, gain):
    rescale = lax.rsqrt(jnp.mean(values * values, axis=1, keepdims=True) + epsilon)
    return (values * rescale * gain).astype(bf16), rescale


def normalize_back(values, gain, rescale, grad):
    weighted = gain * grad
    inner = jnp.sum(values * weighted, axis=1, keepdims=True)
    input_grad = rescale * weighted - values * (rescale * rescale * rescale) / D * inner
    gain_grad = jnp.sum(grad * values * rescale, axis=0, keepdims=True)
    return input_grad, gain_grad


def gelu_parts(v):
    root = 0.7978845608028654
    cubic = 0.044715
    bent = jnp.tanh(root * (v + cubic * (v * v * v)))
    value = 0.5 * v * (1.0 + bent)
    slope = 0.5 * (1.0 + bent) + 0.5 * v * (1.0 - bent * bent) * root * (1.0 + 3.0 * cubic * v * v)
    return value, slope


def sum_over_dp(block, dp_count):
    index = lax.axis_index("dp")
    undo = []
    bit = 1
    while bit < dp_count:
        pairs = [(i, i ^ bit) for i in range(dp_count)]
        rows = block.shape[0]
        side = lax.bitwise_and(lax.div(index, jnp.int32(bit)), jnp.int32(1))
        if rows % 32 == 0:
            low, high = block[: rows // 2], block[rows // 2 :]
            keep = jnp.where(side == 0, low, high)
            send = jnp.where(side == 0, high, low)
            block = (keep.astype(f32) + lax.ppermute(send, "dp", pairs).astype(f32)).astype(bf16)
            undo.append((side, pairs))
        else:
            block = (block.astype(f32) + lax.ppermute(block, "dp", pairs).astype(f32)).astype(bf16)
        bit *= 2
    for side, pairs in reversed(undo):
        other = lax.ppermute(block, "dp", pairs)
        block = jnp.where(
            side == 0,
            jnp.concatenate([block, other], axis=0),
            jnp.concatenate([other, block], axis=0),
        )
    return block


def reduce_group(pieces, dp_count):
    summed = []
    for own, other in pieces:
        arrived = over_col(other)
        summed.append((own.astype(f32) + arrived.astype(f32)).astype(bf16))
    whole = jnp.concatenate(summed, axis=1)
    arrived = over_row(whole[HALF:])
    block = (whole[:HALF].astype(f32) + arrived.astype(f32)).astype(bf16)
    return sum_over_dp(block, dp_count).astype(f32)


def local(
    layer_input,
    encoder_states,
    cotangent,
    buckets,
    gain_self,
    gain_cross,
    gain_ffn,
    self_query,
    self_key,
    self_value,
    self_out,
    cross_query,
    cross_key,
    cross_value,
    cross_out,
    ffn_gate,
    ffn_up,
    ffn_down,
    rel_table,
    dp_count,
):
    r = lax.axis_index("row")
    c = lax.axis_index("col")
    own_small = jnp.concatenate([gain_self, gain_cross, gain_ffn, rel_table.reshape(-1)])
    small = lax.all_gather(own_small, ("row", "col"), axis=0, tiled=False)
    quarter = gain_self.shape[0]
    gains = [
        local_order(small[:, i * quarter : (i + 1) * quarter].reshape(1, D), r, 1) for i in range(3)
    ]
    tables = small[:, 3 * quarter :].reshape(2, 2, 3, NB).transpose(1, 0, 2, 3)
    tables = local_order(tables.reshape(2, 2 * 3, NB), c, 0)
    onehot = (buckets[:, None] == jnp.arange(NB, dtype=jnp.int32)[None, :]).astype(f32)
    placed = jnp.roll(onehot[::-1], LEN - BLK + 1, axis=0)
    bias_rows = lax.dot_general(
        tables.reshape(12, NB), placed, (((1,), (1,)), ((), ())), precision=lax.Precision.HIGHEST
    ).reshape(2, PAIRS, 2, LEN)

    def columns_weight(own):
        mine = jnp.concatenate([own, over_row(own)], axis=0)
        return mine, over_col(mine)

    def rows_weight(own):
        mine = jnp.concatenate([own, over_row(own)], axis=1)
        return mine, over_col(mine)

    self_w = columns_weight(jnp.concatenate([self_query, self_key, self_value], axis=1))
    self_o = rows_weight(self_out)
    cross_kv_w = columns_weight(jnp.concatenate([cross_key, cross_value], axis=1))
    cross_q_w = columns_weight(cross_query)
    cross_o = rows_weight(cross_out)
    ffn_w = columns_weight(jnp.concatenate([ffn_gate, ffn_up], axis=1))
    ffn_d = rows_weight(ffn_down)

    x = local_order(layer_input, r, 1).astype(f32)
    encoder = local_order(encoder_states, r, 1)
    out_grad = local_order(cotangent, r, 1)
    both = range(2)

    normed_one, rescale_one = normalize(x, gains[0])
    qkv = [dot(normed_one, self_w[h]).astype(bf16) for h in both]
    self_att = [
        attention_fwd(qkv[h], 0, qkv[h], PAIRS, qkv[h], 2 * PAIRS, bias_rows[h]) for h in both
    ]
    middle = x + dot(self_att[0][0], self_o[0]) + dot(self_att[1][0], self_o[1])
    normed_two, rescale_two = normalize(middle, gains[1])
    kv = [dot(encoder, cross_kv_w[h]).astype(bf16) for h in both]
    cq = [dot(normed_two, cross_q_w[h]).astype(bf16) for h in both]
    cross_att = [attention_fwd(cq[h], 0, kv[h], 0, kv[h], PAIRS, None) for h in both]
    after = middle + dot(cross_att[0][0], cross_o[0]) + dot(cross_att[1][0], cross_o[1])
    normed_three, rescale_three = normalize(after, gains[2])
    wide = ffn_gate.shape[1]
    gate_up = [dot(normed_three, ffn_w[h]) for h in both]
    parts = [gelu_parts(gate_up[h][:, :wide]) for h in both]
    hidden = [(parts[h][0] * gate_up[h][:, wide:]).astype(bf16) for h in both]
    layer_output = after + dot(hidden[0], ffn_d[0]) + dot(hidden[1], ffn_d[1])

    out_low = out_grad.astype(bf16)
    down_grads = [t_dot(out_low, hidden[h]).astype(bf16) for h in both]
    hidden_grad = [dot_t(out_low, ffn_d[h]) for h in both]
    gate_up_grad = [
        jnp.concatenate(
            [
                (hidden_grad[h] * gate_up[h][:, wide:] * parts[h][1]).astype(bf16),
                (hidden_grad[h] * parts[h][0]).astype(bf16),
            ],
            axis=1,
        )
        for h in both
    ]
    gate_up_w_grads = [t_dot(normed_three, gate_up_grad[h]).astype(bf16) for h in both]
    ffn_sum = reduce_group([gate_up_w_grads, down_grads], dp_count)
    normed_three_grad = dot_t(gate_up_grad[0], ffn_w[0]) + dot_t(gate_up_grad[1], ffn_w[1])
    third, gain_ffn_grad = normalize_back(after, gains[2], rescale_three, normed_three_grad)
    after_grad = out_grad + third

    after_low = after_grad.astype(bf16)
    cross_out_grads = [t_dot(after_low, cross_att[h][0]).astype(bf16) for h in both]
    cross_mixed = [dot_t(after_low, cross_o[h]).astype(bf16) for h in both]
    cross_back = [
        attention_bwd(cq[h], 0, kv[h], 0, kv[h], PAIRS, cross_mixed[h], cross_att[h][1], False)
        for h in both
    ]
    kv_grad = [jnp.concatenate(cross_back[h][1:3], axis=1) for h in both]
    cross_q_grads = [t_dot(normed_two, cross_back[h][0]).astype(bf16) for h in both]
    cross_kv_grads = [t_dot(encoder, kv_grad[h]).astype(bf16) for h in both]
    cross_sum = reduce_group([cross_kv_grads, cross_q_grads, cross_out_grads], dp_count)
    normed_two_grad = dot_t(cross_back[0][0], cross_q_w[0]) + dot_t(cross_back[1][0], cross_q_w[1])
    second, gain_cross_grad = normalize_back(middle, gains[1], rescale_two, normed_two_grad)
    middle_grad = after_grad + second

    middle_low = middle_grad.astype(bf16)
    self_out_grads = [t_dot(middle_low, self_att[h][0]).astype(bf16) for h in both]
    self_mixed = [dot_t(middle_low, self_o[h]).astype(bf16) for h in both]
    self_back = [
        attention_bwd(
            qkv[h], 0, qkv[h], PAIRS, qkv[h], 2 * PAIRS, self_mixed[h], self_att[h][1], True
        )
        for h in both
    ]
    qkv_grad = [jnp.concatenate(self_back[h][:3], axis=1) for h in both]
    self_w_grads = [t_dot(normed_one, qkv_grad[h]).astype(bf16) for h in both]
    self_sum = reduce_group([self_w_grads, self_out_grads], dp_count)
    normed_one_grad = dot_t(qkv_grad[0], self_w[0]) + dot_t(qkv_grad[1], self_w[1])
    first, gain_self_grad = normalize_back(x, gains[0], rescale_one, normed_one_grad)
    input_grad = middle_grad + first

    encoder_grad = dot_t(kv_grad[0], cross_kv_w[0]) + dot_t(kv_grad[1], cross_kv_w[1])

    shift_sums = jnp.stack(
        [jnp.sum(self_back[h][3].reshape(-1, PAIRS * 2, LEN), axis=0) for h in both], axis=0
    )
    table_local = jnp.dot(
        shift_sums.reshape(12, LEN), placed, precision=lax.Precision.HIGHEST
    ).reshape(2, 2, 3, NB)
    table_all = local_order(table_local, c, 0)
    gains_all = local_order(
        jnp.concatenate([gain_self_grad, gain_cross_grad, gain_ffn_grad], axis=0), r, 1
    )
    small_all = lax.psum(
        jnp.concatenate([gains_all.reshape(-1), table_all.reshape(-1)]), ("dp", "row", "col")
    )
    gains_sum = small_all[: 3 * D].reshape(3, D)
    table_sum = small_all[3 * D :].reshape(2, 2, 3, NB)
    start = (r * 2 + c) * quarter
    gains_own = lax.dynamic_slice_in_dim(gains_sum, start, quarter, 1)
    table_own = lax.dynamic_slice(table_sum, (c, r, 0, 0), (1, 1, 3, NB))

    hw = self_query.shape[1]
    back_order = lambda v: local_order(v, r, 1)
    return (
        back_order(layer_output),
        back_order(input_grad),
        back_order(encoder_grad),
        gains_own[0],
        gains_own[1],
        gains_own[2],
        self_sum[:, :hw],
        self_sum[:, hw : 2 * hw],
        self_sum[:, 2 * hw : 3 * hw],
        self_sum[:, 3 * hw :].T,
        cross_sum[:, 2 * hw : 3 * hw],
        cross_sum[:, :hw],
        cross_sum[:, hw : 2 * hw],
        cross_sum[:, 3 * hw :].T,
        ffn_sum[:, :wide],
        ffn_sum[:, wide : 2 * wide],
        ffn_sum[:, 2 * wide :].T,
        table_own,
    )


def solution(mesh):
    tokens = P(("dp", "row", "col"), None)
    gain = P(("row", "col"))
    columns = P("row", "col")
    rows = P("col", "row")
    table = P("col", "row", None, None)
    weights = (columns,) * 3 + (rows,) + (columns,) * 3 + (rows,) + (columns,) * 2 + (rows,)
    in_specs = (tokens,) * 3 + (P(),) + (gain,) * 3 + weights + (table,)
    out_specs = (tokens,) * 3 + (gain,) * 3 + weights + (table,)
    body = functools.partial(local, dp_count=mesh.shape["dp"])
    return jax.shard_map(
        body, mesh=mesh, in_specs=in_specs, out_specs=out_specs, check_vma=False
    )
```

```python
import functools

import jax
import jax.numpy as jnp
from jax import lax
from jax.experimental import pallas as pl
from jax.experimental.pallas import tpu as pltpu
from jax.sharding import PartitionSpec as P

D = 768
HD = 64
NB = 32
LEN = 512
BLK = 256
HALF = D // 2
PAIRS = HALF // (2 * HD)

epsilon = 1e-06
masked_score = -1e30
f32 = jnp.float32
bf16 = jnp.bfloat16
SWAP = [(0, 1), (1, 0)]


def over_row(x):
    return lax.ppermute(x, "row", SWAP)


def over_col(x):
    return lax.ppermute(x, "col", SWAP)


def dot(a, b):
    return jnp.dot(a, b, preferred_element_type=f32)


def dot_t(a, b):
    return lax.dot_general(a, b, (((1,), (1,)), ((), ())), preferred_element_type=f32)


def t_dot(a, b):
    return lax.dot_general(a, b, (((0,), (0,)), ((), ())), preferred_element_type=f32)


def pin(*values):
    return lax.optimization_barrier(values)


def local_order(x, flag, axis):
    first, second = jnp.split(x, 2, axis=axis)
    swapped = jnp.concatenate([second, first], axis=axis)
    return jnp.where(flag == 0, x, swapped)


def causal_mask():
    rows = lax.broadcasted_iota(jnp.int32, (BLK, BLK), 0)
    cols = lax.broadcasted_iota(jnp.int32, (BLK, BLK), 1)
    return rows >= cols


def softmax_rows(scores):
    top = jnp.max(scores, axis=1, keepdims=True)
    shifted = jnp.exp(scores - top)
    total = jnp.sum(shifted, axis=1, keepdims=True)
    return (shifted * (1.0 / total)).astype(bf16)


def self_fwd_kernel(q_ref, k_ref, v_ref, bias_ref, out_ref, probs_ref):
    mask = causal_mask()
    for head in range(2):
        lanes = slice(head * HD, (head + 1) * HD)
        row = jnp.broadcast_to(bias_ref[0, head : head + 1, :], (BLK, LEN))
        bias = pltpu.roll(row, 0, 1, stride=1, stride_axis=0)
        for block in range(LEN // BLK):
            rows = slice(block * BLK, (block + 1) * BLK)
            wide = (block + 1) * BLK
            scores = dot_t(q_ref[rows, lanes], k_ref[:wide, lanes])
            scores = scores + bias[:, LEN - wide :]
            last = jnp.where(mask, scores[:, wide - BLK :], masked_score)
            if block:
                scores = jnp.concatenate([scores[:, : wide - BLK], last], axis=1)
            else:
                scores = last
            probs = softmax_rows(scores)
            probs_ref[head, rows, :wide] = probs
            out_ref[rows, lanes] = dot(probs, v_ref[:wide, lanes]).astype(bf16)


def cross_fwd_kernel(q_ref, k_ref, v_ref, out_ref, probs_ref):
    for head in range(2):
        lanes = slice(head * HD, (head + 1) * HD)
        probs = softmax_rows(dot_t(q_ref[:, lanes], k_ref[:, lanes]))
        probs_ref[head] = probs
        out_ref[:, lanes] = dot(probs, v_ref[:, lanes]).astype(bf16)


def score_grad_of(probs, weight_grads):
    wide = probs.astype(f32)
    mixed = wide * weight_grads
    inner = jnp.sum(mixed, axis=1, keepdims=True)
    return mixed - wide * inner


def shift_sum(total):
    acc = total[:8]
    for first in range(8, BLK, 8):
        acc = acc + pltpu.roll(total[first : first + 8], LEN - first, 1)
    line = lax.broadcasted_iota(jnp.int32, (8, LEN), 0)
    for bit in (1, 2, 4):
        acc = jnp.where((line & bit) != 0, pltpu.roll(acc, LEN - bit, 1), acc)
    return jnp.sum(acc, axis=0, keepdims=True)


def self_bwd_kernel(q_ref, k_ref, v_ref, g_ref, probs_ref, dq_ref, dk_ref, dv_ref, shift_ref, ds_ref):
    for head in range(2):
        lanes = slice(head * HD, (head + 1) * HD)
        total = jnp.zeros((BLK, LEN), f32)
        for block in range(LEN // BLK):
            rows = slice(block * BLK, (block + 1) * BLK)
            wide = (block + 1) * BLK
            weight_grads = dot_t(g_ref[rows, lanes], v_ref[:wide, lanes])
            grads = score_grad_of(probs_ref[head, rows, :wide], weight_grads)
            if wide < LEN:
                total = total + jnp.concatenate([jnp.zeros((BLK, LEN - wide), f32), grads], axis=1)
            else:
                total = total + grads
            short = grads.astype(bf16)
            ds_ref[rows, :wide] = short
            dq_ref[rows, lanes] = dot(short, k_ref[:wide, lanes]).astype(bf16)
        for block in range(LEN // BLK):
            cols = slice(block * BLK, (block + 1) * BLK)
            rest = slice(block * BLK, LEN)
            dk_ref[cols, lanes] = t_dot(ds_ref[rest, cols], q_ref[rest, lanes]).astype(bf16)
            dv_ref[cols, lanes] = t_dot(probs_ref[head, rest, cols], g_ref[rest, lanes]).astype(bf16)
        shift_ref[0, head : head + 1, :] = shift_sum(total)


def cross_bwd_kernel(q_ref, k_ref, v_ref, g_ref, probs_ref, dq_ref, dk_ref, dv_ref):
    for head in range(2):
        lanes = slice(head * HD, (head + 1) * HD)
        weight_grads = dot_t(g_ref[:, lanes], v_ref[:, lanes])
        short = score_grad_of(probs_ref[head], weight_grads).astype(bf16)
        dq_ref[:, lanes] = dot(short, k_ref[:, lanes]).astype(bf16)
        dk_ref[:, lanes] = t_dot(short, q_ref[:, lanes]).astype(bf16)
        dv_ref[:, lanes] = t_dot(probs_ref[head], g_ref[:, lanes]).astype(bf16)


def lane_block(first):
    return pl.BlockSpec((LEN, 2 * HD), lambda s, g: (s, first + g))


PROBS = pl.BlockSpec((2, LEN, LEN), lambda s, g: (s * PAIRS + g, 0, 0))
BIAS = pl.BlockSpec((1, 2, LEN), lambda s, g: (g, 0, 0))
SHIFT = pl.BlockSpec((1, 2, LEN), lambda s, g: (s * PAIRS + g, 0, 0))


def cost(flops, moved):
    return pl.CostEstimate(flops=flops, bytes_accessed=moved, transcendentals=0)


def attention_fwd(queries, query_at, keys, key_at, values, value_at, bias):
    tokens = queries.shape[0]
    sequences = tokens // LEN
    specs = [lane_block(query_at), lane_block(key_at), lane_block(value_at)]
    operands = [queries, keys, values]
    if bias is not None:
        specs.append(BIAS)
        operands.append(bias)
    return pl.pallas_call(
        cross_fwd_kernel if bias is None else self_fwd_kernel,
        grid=(sequences, PAIRS),
        in_specs=specs,
        out_specs=[lane_block(0), PROBS],
        out_shape=[
            jax.ShapeDtypeStruct((tokens, HALF), bf16),
            jax.ShapeDtypeStruct((sequences * PAIRS * 2, LEN, LEN), bf16),
        ],
        cost_estimate=cost(4 * tokens * LEN * HALF * 4, tokens * LEN * 12),
    )(*operands)


def attention_bwd(queries, query_at, keys, key_at, values, value_at, grads, probs, causal):
    tokens = queries.shape[0]
    sequences = tokens // LEN
    piece = jax.ShapeDtypeStruct((tokens, HALF), bf16)
    out_shape = [piece] * 3
    out_specs = [lane_block(0)] * 3
    if causal:
        out_shape.append(jax.ShapeDtypeStruct((sequences * PAIRS, 2, LEN), f32))
        out_specs.append(SHIFT)
    return pl.pallas_call(
        self_bwd_kernel if causal else cross_bwd_kernel,
        grid=(sequences, PAIRS),
        in_specs=[lane_block(query_at), lane_block(key_at), lane_block(value_at), lane_block(0), PROBS],
        out_specs=out_specs,
        out_shape=out_shape,
        scratch_shapes=[pltpu.VMEM((LEN, LEN), bf16)] if causal else [],
        cost_estimate=cost(8 * tokens * LEN * HALF * 4, tokens * LEN * 12),
    )(queries, keys, values, grads, probs)


def halves(ref, r):
    first = ref[:, pl.ds(pl.multiple_of(r * HALF, 128), HALF)]
    second = ref[:, pl.ds(pl.multiple_of((1 - r) * HALF, 128), HALF)]
    return jnp.concatenate([first, second], axis=1)


def store_halves(ref, r, value):
    ref[:, pl.ds(pl.multiple_of(r * HALF, 128), HALF)] = value[:, :HALF]
    ref[:, pl.ds(pl.multiple_of((1 - r) * HALF, 128), HALF)] = value[:, HALF:]


def rescale_of(values):
    return lax.rsqrt(jnp.mean(values * values, axis=1, keepdims=True) + epsilon)


def norm_back(values, gain, grad):
    rescale = rescale_of(values)
    weighted = gain * grad
    inner = jnp.sum(values * weighted, axis=1, keepdims=True)
    input_grad = rescale * weighted - values * (rescale * rescale * rescale) / D * inner
    return input_grad, jnp.sum(grad * values * rescale, axis=0, keepdims=True)


def tall(low_ref, high_ref):
    return jnp.concatenate([low_ref[...], high_ref[...]], axis=0)


def broad(low_ref, high_ref):
    return jnp.concatenate([low_ref[...], high_ref[...]], axis=1)


def stack_kernel(*refs):
    out = refs[-1]
    for i, ref in enumerate(refs[:-1]):
        out[i * ref.shape[0] : (i + 1) * ref.shape[0], :] = ref[...]


def stacked(*parts):
    shape = (sum(p.shape[0] for p in parts), parts[0].shape[1])
    return call(
        stack_kernel, list(parts), [whole(p.shape) for p in parts], shaped(*shape, dtype=bf16), whole(shape)
    )


def pre_self_kernel(r_ref, x_ref, gain_ref, w00, w10, w01, w11, n_ref, x32_ref, own_ref, other_ref):
    @pl.when(pl.program_id(0) == 0)
    def _():
        values = halves(x_ref, r_ref[0]).astype(f32)
        x32_ref[...] = values
        n_ref[...] = (values * rescale_of(values) * gain_ref[...]).astype(bf16)

    own_ref[...] = dot(n_ref[...], tall(w00, w10)).astype(bf16)
    other_ref[...] = dot(n_ref[...], tall(w01, w11)).astype(bf16)


def encoder_kernel(r_ref, x_ref, w00, w10, w01, w11, x_out_ref, own_ref, other_ref):
    @pl.when(pl.program_id(0) == 0)
    def _():
        x_out_ref[...] = halves(x_ref, r_ref[0])

    own_ref[...] = dot(x_out_ref[...], tall(w00, w10)).astype(bf16)
    other_ref[...] = dot(x_out_ref[...], tall(w01, w11)).astype(bf16)


def join_kernel(base_ref, a0, a1, o00, o10, o01, o11, gain_ref, *rest):
    out_ref, n_ref = rest[-4:-2] if len(rest) > 2 else rest
    value = base_ref[...] + dot(a0[...], broad(o00, o10)) + dot(a1[...], broad(o01, o11))
    out_ref[...] = value
    normed = (value * rescale_of(value) * gain_ref[...]).astype(bf16)
    n_ref[...] = normed
    if len(rest) > 2:
        q00, q10, q01, q11 = rest[:4]
        rest[-2][...] = dot(normed, tall(q00, q10)).astype(bf16)
        rest[-1][...] = dot(normed, tall(q01, q11)).astype(bf16)


def gelu_parts(v):
    root = 0.7978845608028654
    cubic = 0.044715
    bent = jnp.tanh(root * (v + cubic * (v * v * v)))
    value = 0.5 * v * (1.0 + bent)
    slope = 0.5 * (1.0 + bent) + 0.5 * v * (1.0 - bent * bent) * root * (1.0 + 3.0 * cubic * v * v)
    return value, slope


def ffn_kernel(first, r_ref, n_ref, cot_ref, out_in, ng_in, g0, g1, u0, u1, d0, d1, out_ref, ng_ref, low_ref, dg_ref, du_ref, dd_ref, nt_ref, lt_ref):
    @pl.when(pl.program_id(0) == 0)
    def _():
        if first:
            low = halves(cot_ref, r_ref[0]).astype(bf16)
            out_ref[...] = out_in[...]
            ng_ref[...] = jnp.zeros_like(ng_ref)
        else:
            low = cot_ref[...]
            out_ref[...] = out_in[...]
            ng_ref[...] = ng_in[...]
        low_ref[...] = low
        nt_ref[...] = n_ref[...].T
        lt_ref[...] = low.T

    normed = n_ref[...]
    gate_w, up_w, down_w = tall(g0, g1), tall(u0, u1), broad(d0, d1)
    gate = dot(normed, gate_w)
    up = dot(normed, up_w)
    hidden_grad = dot_t(low_ref[...], down_w)
    value, slope = gelu_parts(gate)
    hidden = (value * up).astype(bf16)
    gate_grad = (hidden_grad * up * slope).astype(bf16)
    up_grad = (hidden_grad * value).astype(bf16)
    out_ref[...] += dot(hidden, down_w)
    ng_ref[...] += dot_t(gate_grad, gate_w) + dot_t(up_grad, up_w)
    dg_ref[...] = dot(nt_ref[...], gate_grad).astype(bf16)
    du_ref[...] = dot(nt_ref[...], up_grad).astype(bf16)
    dd_ref[...] = dot(lt_ref[...], hidden).astype(bf16)


def after_ffn_kernel(r_ref, after_ref, cot_ref, ng_ref, gain_ref, o00, o10, o01, o11, grad_ref, low_ref, m0, m1, gg_ref):
    third, gain_grad = norm_back(after_ref[...], gain_ref[...], ng_ref[...])
    gg_ref[...] = gain_grad
    total = halves(cot_ref, r_ref[0]) + third
    grad_ref[...] = total
    low = total.astype(bf16)
    low_ref[...] = low
    m0[...] = dot_t(low, broad(o00, o10)).astype(bf16)
    m1[...] = dot_t(low, broad(o01, o11)).astype(bf16)


def after_cross_kernel(middle_ref, base_ref, dq0, dq1, q00, q10, q01, q11, gain_ref, o00, o10, o01, o11, grad_ref, low_ref, m0, m1, gg_ref):
    normed_grad = dot_t(dq0[...], tall(q00, q10)) + dot_t(dq1[...], tall(q01, q11))
    second, gain_grad = norm_back(middle_ref[...], gain_ref[...], normed_grad)
    gg_ref[...] = gain_grad
    total = base_ref[...] + second
    grad_ref[...] = total
    low = total.astype(bf16)
    low_ref[...] = low
    m0[...] = dot_t(low, broad(o00, o10)).astype(bf16)
    m1[...] = dot_t(low, broad(o01, o11)).astype(bf16)


def weight_grad_kernel(shared, *refs):
    lefts = max(shared) + 1
    turned = [refs[i][...].T for i in range(lefts)]
    out = refs[-1]
    for place, left in enumerate(shared):
        right = refs[lefts + place][...]
        out[:, place * HALF : (place + 1) * HALF] = dot(turned[left], right).astype(bf16)


def input_grad_kernel(r_ref, x_ref, base_ref, gain_ref, *refs):
    own, other, w = refs[:3], refs[3:6], refs[6:18]
    out_ref, gg_ref = refs[18:]
    normed_grad = 0.0
    for j in range(3):
        w00, w10, w01, w11 = w[4 * j : 4 * j + 4]
        normed_grad = normed_grad + dot_t(own[j][...], tall(w00, w10)) + dot_t(other[j][...], tall(w01, w11))
    first, gain_grad = norm_back(x_ref[...], gain_ref[...], normed_grad)
    gg_ref[...] = gain_grad
    store_halves(out_ref, r_ref[0], base_ref[...] + first)


def encoder_grad_kernel(r_ref, out_in, k0, v0, k1, v1, *refs):
    w, (out_ref, layer_ref) = refs[:8], refs[8:]
    total = 0.0
    for j, (own, other) in enumerate(((k0, k1), (v0, v1))):
        w00, w10, w01, w11 = w[4 * j : 4 * j + 4]
        total = total + dot_t(own[...], tall(w00, w10)) + dot_t(other[...], tall(w01, w11))
    store_halves(out_ref, r_ref[0], total)
    store_halves(layer_ref, r_ref[0], out_in[...])


SCALAR = pl.BlockSpec(memory_space=pltpu.SMEM)


def whole(shape):
    return pl.BlockSpec(shape, lambda *grid: (0,) * len(shape))


def square(row):
    return pl.BlockSpec((HALF, HALF), lambda *grid: (row, 0))


def moving(first):
    return pl.BlockSpec((HALF, HALF), lambda j: (first + j, 0))


def shaped(*shape, dtype=f32):
    return jax.ShapeDtypeStruct(shape, dtype)


def call(kernel, operands, in_specs, out_shape, out_specs, grid=(1,), scratch=(), flops=0):
    moved = sum(x.size * x.dtype.itemsize for x in operands)
    return pl.pallas_call(
        kernel,
        grid=grid,
        in_specs=in_specs,
        out_specs=out_specs,
        out_shape=out_shape,
        scratch_shapes=list(scratch),
        cost_estimate=cost(flops, moved),
        compiler_params=pltpu.CompilerParams(vmem_limit_bytes=56 << 20),
    )(*operands)


def added(a, b):
    return (a.astype(f32) + b.astype(f32)).astype(bf16)


class Reducer:
    def __init__(self, dp_count, own, arrived, cut):
        self.dp_count = dp_count
        self.index = lax.axis_index("dp")
        self.undo = []
        self.cut = cut
        self.split = dp_count % 2 == 0
        whole_group = jnp.concatenate([added(a, b) for a, b in zip(own, arrived)], axis=1)
        if not self.split:
            cut = whole_group.shape[1]
        left, right = whole_group[:, :cut], whole_group[:, cut:]
        self.keep_left, self.send_left = left[:HALF], left[HALF:]
        if self.split:
            quarter = HALF // 2
            right = right.reshape(2, 2, quarter, right.shape[1])
            side = self.side(1)
            self.keep_right = jnp.where(side == 0, right[:, 0], right[:, 1])
            self.send_right = jnp.where(side == 0, right[:, 1], right[:, 0])

    def side(self, bit):
        return lax.bitwise_and(lax.div(self.index, jnp.int32(bit)), jnp.int32(1))

    def over(self, bit, x):
        return lax.ppermute(x, "dp", [(i, i ^ bit) for i in range(self.dp_count)])

    def first(self):
        self.came_left = over_row(self.send_left)
        if self.split:
            self.came_right = self.over(1, self.send_right)
            return self.came_left, self.came_right
        return (self.came_left,)

    def second(self, came):
        left = added(self.keep_left, came[0])
        if not self.split:
            self.block = left
            return ()
        quarter = HALF // 2
        side = self.side(1)
        low, high = left[:quarter], left[quarter:]
        self.keep_left = jnp.where(side == 0, low, high)
        right = added(self.keep_right, came[1])
        self.keep_right = right[0]
        self.undo.append(1)
        return self.over(1, jnp.where(side == 0, high, low)), over_row(right[1])

    def join(self, came):
        if self.split:
            self.block = jnp.concatenate(
                [added(self.keep_left, came[0]), added(self.keep_right, came[1])], axis=1
            )

    def bits(self):
        bit = 2 if self.split else 1
        while bit < self.dp_count:
            yield bit
            bit *= 2

    def down_start(self, bit):
        rows = self.block.shape[0]
        if rows % 32 == 0:
            side = self.side(bit)
            low, high = self.block[: rows // 2], self.block[rows // 2 :]
            self.block = jnp.where(side == 0, low, high)
            self.undo.append(bit)
            return self.over(bit, jnp.where(side == 0, high, low))
        return self.over(bit, self.block)

    def down_end(self, came):
        self.block = added(self.block, came)

    def down(self):
        for bit in self.bits():
            self.down_end(self.down_start(bit))

    def up(self):
        for bit in reversed(self.undo):
            other = self.over(bit, self.block)
            self.block = jnp.where(
                self.side(bit) == 0,
                jnp.concatenate([self.block, other], axis=0),
                jnp.concatenate([other, self.block], axis=0),
            )
        return self.block.astype(f32)


def local(
    layer_input,
    encoder_states,
    cotangent,
    buckets,
    gain_self,
    gain_cross,
    gain_ffn,
    self_query,
    self_key,
    self_value,
    self_out,
    cross_query,
    cross_key,
    cross_value,
    cross_out,
    ffn_gate,
    ffn_up,
    ffn_down,
    rel_table,
    dp_count,
):
    r = lax.axis_index("row")
    c = lax.axis_index("col")
    own_small = jnp.concatenate([gain_self, gain_cross, gain_ffn, rel_table.reshape(-1)])
    quarter = gain_self.shape[0]
    by_row = jnp.stack([own_small, over_row(own_small)], axis=0)
    by_both = jnp.stack([by_row, over_col(by_row)], axis=1)
    by_col = local_order(by_both, c, 1)
    gains = [by_col[:, :, i * quarter : (i + 1) * quarter].reshape(1, D) for i in range(3)]
    tables = local_order(by_both, r, 0)[:, :, 3 * quarter :].transpose(1, 0, 2)
    onehot = (buckets[:, None] == jnp.arange(NB, dtype=jnp.int32)[None, :]).astype(f32)
    placed = jnp.roll(onehot[::-1], LEN - BLK + 1, axis=0)
    bias_rows = lax.dot_general(
        tables.reshape(12, NB), placed, (((1,), (1,)), ((), ())), precision=lax.Precision.HIGHEST
    ).reshape(2, PAIRS, 2, LEN)

    tokens = layer_input.shape[0]
    row_index = jnp.reshape(r, (1,))
    both = range(2)
    tok = whole((tokens, D))
    tok_half = whole((tokens, HALF))
    vec = whole((1, D))
    tok_f32, tok_bf16 = shaped(tokens, D), shaped(tokens, D, dtype=bf16)
    half_bf16 = shaped(tokens, HALF, dtype=bf16)
    dense = 2 * tokens * D * HALF

    def gathered(own, arrived):
        return [own, arrived, over_col(own), over_col(arrived)]

    msg_self = stacked(self_query, self_key, self_value)
    got_self = over_row(msg_self)
    w_self = gathered(msg_self, got_self)
    msg_mid = stacked(self_out, cross_query, cross_key, cross_value, cross_out)
    msg_mid, got_self = pin(msg_mid, got_self)
    got_mid = over_row(msg_mid)
    so, cqw, ckw, cvw, cow = range(5)
    part = shaped(tokens, 3 * HALF, dtype=bf16)
    normed_one, x, qkv_own, qkv_other = call(
        pre_self_kernel,
        [row_index, layer_input, gains[0]] + w_self,
        [SCALAR, tok, vec] + [moving(0)] * 4,
        [tok_bf16, tok_f32, part, part],
        [tok, tok] + [pl.BlockSpec((tokens, HALF), lambda j: (0, j))] * 2,
        grid=(3,),
        flops=6 * dense,
    )
    qkv = [qkv_own, qkv_other]
    self_att = [
        list(attention_fwd(qkv[h], 0, qkv[h], PAIRS, qkv[h], 2 * PAIRS, bias_rows[h])) for h in both
    ]
    msg_up = stacked(ffn_gate, ffn_up)
    self_att, got_mid, msg_up, msg_down = pin(self_att, got_mid, msg_up, ffn_down)
    got_up = over_row(msg_up)
    w_mid = gathered(msg_mid, got_mid)

    part = shaped(tokens, 2 * HALF, dtype=bf16)
    encoder, kv_own, kv_other = call(
        encoder_kernel,
        [row_index, encoder_states] + w_mid,
        [SCALAR, tok] + [moving(ckw)] * 4,
        [tok_bf16, part, part],
        [tok] + [pl.BlockSpec((tokens, HALF), lambda j: (0, j))] * 2,
        grid=(2,),
        flops=4 * dense,
    )
    kv = [kv_own, kv_other]
    middle, normed_two, cq_own, cq_other = call(
        join_kernel,
        [x, self_att[0][0], self_att[1][0]] + w_mid + [gains[1]] + w_mid,
        [tok, tok_half, tok_half] + [square(so)] * 4 + [vec] + [square(cqw)] * 4,
        [tok_f32, tok_bf16, half_bf16, half_bf16],
        [tok, tok, tok_half, tok_half],
        flops=4 * dense,
    )
    cq = [cq_own, cq_other]
    cq, kv, msg_down = pin(cq, kv, msg_down)
    got_down = over_row(msg_down)
    cross_att = [attention_fwd(cq[h], 0, kv[h], 0, kv[h], PAIRS, None) for h in both]
    cross_att, got_up = pin(cross_att, got_up)
    w_up = gathered(msg_up, got_up)
    w_down = gathered(msg_down, got_down)
    after, normed_three = call(
        join_kernel,
        [middle, cross_att[0][0], cross_att[1][0]] + w_mid + [gains[2]],
        [tok, tok_half, tok_half] + [square(cow)] * 4 + [vec],
        [tok_f32, tok_bf16],
        [tok, tok],
        flops=2 * dense,
    )

    width = ffn_gate.shape[1]
    tile = 256
    up_tile = lambda first: pl.BlockSpec((HALF, tile), lambda t: (first, t))
    down_tile = pl.BlockSpec((tile, HALF), lambda t: (t, 0))
    grad_tile = pl.BlockSpec((D, tile), lambda t: (0, t))
    grad_shape = shaped(D, width, dtype=bf16)
    layer_local, ng, out_low = after, after, cotangent
    ffn_grads = [None, None]
    for h in both:
        lo, hi = w_up[2 * h], w_up[2 * h + 1]
        layer_local, ng, out_low, *ffn_grads[h] = call(
            functools.partial(ffn_kernel, h == 0),
            [row_index, normed_three, out_low, layer_local, ng, lo, hi, lo, hi, w_down[2 * h], w_down[2 * h + 1]],
            [SCALAR] + [tok] * 4 + [up_tile(0)] * 2 + [up_tile(1)] * 2 + [down_tile] * 2,
            [tok_f32, tok_f32, tok_bf16] + [grad_shape] * 3,
            [tok] * 3 + [grad_tile] * 3,
            grid=(width // tile,),
            scratch=[pltpu.VMEM((D, tokens), bf16)] * 2,
            flops=9 * 2 * tokens * D * width,
        )
    after_grad, after_low, mixed_own, mixed_other, gain_ffn_grad = call(
        after_ffn_kernel,
        [row_index, after, cotangent, ng, gains[2]] + w_mid,
        [SCALAR, tok, tok, tok, vec] + [square(cow)] * 4,
        [tok_f32, tok_bf16, half_bf16, half_bf16, shaped(1, D)],
        [tok, tok, tok_half, tok_half, vec],
        flops=2 * dense,
    )
    cross_mixed = [mixed_own, mixed_other]
    ffn_came = [over_col(g) for g in ffn_grads[1]]

    cross_back = [None, None]
    cross_back[1] = attention_bwd(
        cq[1], 0, kv[1], 0, kv[1], PAIRS, cross_mixed[1], cross_att[1][1], False
    )
    cross_back[1], cross_mixed[0], ffn_came = pin(cross_back[1], cross_mixed[0], ffn_came)
    ffn = Reducer(dp_count, ffn_grads[0], ffn_came, 3 * width // 2)
    ffn.keep_left, ffn.send_left, ffn.keep_right, ffn.send_right, cross_mixed[0] = pin(
        ffn.keep_left, ffn.send_left, ffn.keep_right, ffn.send_right, cross_mixed[0]
    )
    ffn_came = ffn.first()
    cross_back[0] = attention_bwd(
        cq[0], 0, kv[0], 0, kv[0], PAIRS, cross_mixed[0], cross_att[0][1], False
    )
    middle_grad, middle_low, mixed_own, mixed_other, gain_cross_grad = call(
        after_cross_kernel,
        [middle, after_grad, cross_back[0][0], cross_back[1][0]] + w_mid + [gains[1]] + w_mid,
        [tok, tok, tok_half, tok_half] + [square(cqw)] * 4 + [vec] + [square(so)] * 4,
        [tok_f32, tok_bf16, half_bf16, half_bf16, shaped(1, D)],
        [tok, tok, tok_half, tok_half, vec],
        flops=4 * dense,
    )
    self_mixed = [mixed_own, mixed_other]
    cross_grads = [
        call(
            functools.partial(weight_grad_kernel, (0, 0, 1, 2, 3)),
            [encoder, normed_two, after_low, middle_low]
            + [cross_back[h][1], cross_back[h][2], cross_back[h][0], cross_att[h][0], self_att[h][0]],
            [tok] * 4 + [tok_half] * 5,
            shaped(D, 5 * HALF, dtype=bf16),
            whole((D, 5 * HALF)),
            flops=5 * dense,
        )
        for h in both
    ]
    self_mixed, cross_grads, ffn_came = pin(self_mixed, cross_grads, ffn_came)
    cross_came = over_col(cross_grads[1])
    ffn_came = ffn.second(ffn_came)

    self_back = [None, None]
    self_back[1] = attention_bwd(
        qkv[1], 0, qkv[1], PAIRS, qkv[1], 2 * PAIRS, self_mixed[1], self_att[1][1], True
    )
    self_back[1], self_mixed[0], ffn_came, cross_came = pin(
        self_back[1], self_mixed[0], ffn_came, cross_came
    )
    ffn.join(ffn_came)
    cross = Reducer(dp_count, [cross_grads[0]], [cross_came], 1024)
    cross_came = cross.first()
    waiting = list(ffn.bits())
    ffn_came = ffn.down_start(waiting[0]) if waiting else ()
    self_back[0] = attention_bwd(
        qkv[0], 0, qkv[0], PAIRS, qkv[0], 2 * PAIRS, self_mixed[0], self_att[0][1], True
    )
    self_grads = [
        call(
            functools.partial(weight_grad_kernel, (0, 0, 0)),
            [normed_one] + list(self_back[h][:3]),
            [tok] + [tok_half] * 3,
            shaped(D, 3 * HALF, dtype=bf16),
            whole((D, 3 * HALF)),
            flops=3 * dense,
        )
        for h in both
    ]
    self_grads, ffn_came, cross_came, middle_grad, layer_local = pin(
        self_grads, ffn_came, cross_came, middle_grad, layer_local
    )
    self_came = over_col(self_grads[1])
    if waiting:
        ffn.down_end(ffn_came)
        for bit in waiting[1:]:
            ffn.down_end(ffn.down_start(bit))
    cross_came = cross.second(cross_came)
    own = Reducer(dp_count, [self_grads[0]], [self_came], 512)
    self_came = own.first()
    cross.join(cross_came)
    cross.down()
    self_came = own.second(self_came)
    own.join(self_came)
    own.down()
    ffn_sum = ffn.up()
    cross_sum = cross.up()
    self_sum = own.up()
    input_grad, gain_self_grad = call(
        input_grad_kernel,
        [row_index, x, middle_grad, gains[0]] + list(self_back[0][:3]) + list(self_back[1][:3]) + w_self * 3,
        [SCALAR, tok, tok, vec] + [tok_half] * 6 + [square(j) for j in range(3) for _ in range(4)],
        [tok_f32, shaped(1, D)],
        [tok, vec],
        flops=6 * dense,
    )
    encoder_grad, layer_output = call(
        encoder_grad_kernel,
        [row_index, layer_local] + list(cross_back[0][1:3]) + list(cross_back[1][1:3]) + w_mid * 2,
        [SCALAR, tok] + [tok_half] * 4 + [square(j) for j in (ckw, cvw) for _ in range(4)],
        [tok_f32, tok_f32],
        [tok, tok],
        flops=4 * dense,
    )

    shift_sums = jnp.stack(
        [jnp.sum(self_back[h][3].reshape(-1, PAIRS * 2, LEN), axis=0) for h in both], axis=0
    )
    table_local = jnp.dot(
        shift_sums.reshape(12, LEN), placed, precision=lax.Precision.HIGHEST
    ).reshape(2, 2, 3 * NB)
    table_local = local_order(table_local, r, 1).transpose(1, 0, 2)
    gains_local = jnp.stack([gain_self_grad, gain_cross_grad, gain_ffn_grad], axis=0)
    gains_local = local_order(gains_local.reshape(3, 2, 2, quarter), c, 2)
    gains_local = gains_local.transpose(1, 2, 0, 3).reshape(2, 2, 3 * quarter)
    small = jnp.concatenate([gains_local, table_local], axis=2)
    small = small[:, 0] + over_col(small[:, 1])
    small = small[0] + over_row(small[1])
    bit = 1
    while bit < dp_count:
        small = small + lax.ppermute(small, "dp", [(i, i ^ bit) for i in range(dp_count)])
        bit *= 2
    gains_own = small[: 3 * quarter].reshape(3, quarter)
    table_own = small[3 * quarter :].reshape(1, 1, 3, NB)

    def column(block, at):
        return block[:, at * HALF : (at + 1) * HALF]

    return (
        layer_output,
        input_grad,
        encoder_grad,
        gains_own[0],
        gains_own[1],
        gains_own[2],
        column(self_sum, 0),
        column(self_sum, 1),
        column(self_sum, 2),
        column(cross_sum, 4).T,
        column(cross_sum, 2),
        column(cross_sum, 0),
        column(cross_sum, 1),
        column(cross_sum, 3).T,
        ffn_sum[:, :width],
        ffn_sum[:, width : 2 * width],
        ffn_sum[:, 2 * width :].T,
        table_own,
    )


def solution(mesh):
    tokens = P(("dp", "row", "col"), None)
    gain = P(("row", "col"))
    columns = P("row", "col")
    rows = P("col", "row")
    table = P("col", "row", None, None)
    weights = (columns,) * 3 + (rows,) + (columns,) * 3 + (rows,) + (columns,) * 2 + (rows,)
    in_specs = (tokens,) * 3 + (P(),) + (gain,) * 3 + weights + (table,)
    out_specs = (tokens,) * 3 + (gain,) * 3 + weights + (table,)
    body = functools.partial(local, dp_count=mesh.shape["dp"])
    return jax.shard_map(
        body, mesh=mesh, in_specs=in_specs, out_specs=out_specs, check_vma=False
    )
```

```python
import functools

import jax
import jax.numpy as jnp
from jax import lax
from jax.experimental import pallas as pl
from jax.experimental.pallas import tpu as pltpu
from jax.sharding import PartitionSpec as P

D = 768
HD = 64
NB = 32
LEN = 512
BLK = 256
HALF = D // 2
PAIRS = D // (2 * HD)

epsilon = 1e-06
masked_score = -1e30
f32 = jnp.float32
bf16 = jnp.bfloat16
SWAP = [(0, 1), (1, 0)]


def over_row(x):
    return lax.ppermute(x, "row", SWAP)


def over_col(x):
    return lax.ppermute(x, "col", SWAP)


def dot(a, b):
    return jnp.dot(a, b, preferred_element_type=f32)


def dot_t(a, b):
    return lax.dot_general(a, b, (((1,), (1,)), ((), ())), preferred_element_type=f32)


def t_dot(a, b):
    return lax.dot_general(a, b, (((0,), (0,)), ((), ())), preferred_element_type=f32)


def pin(*values):
    return lax.optimization_barrier(values)


def _pinned(values):
    present = [v for v in values if v is not None]
    held = list(pin(*present))
    return [None if v is None else held.pop(0) for v in values]


def local_order(x, flag, axis):
    first, second = jnp.split(x, 2, axis=axis)
    swapped = jnp.concatenate([second, first], axis=axis)
    return jnp.where(flag == 0, x, swapped)


def causal_mask():
    rows = lax.broadcasted_iota(jnp.int32, (BLK, BLK), 0)
    cols = lax.broadcasted_iota(jnp.int32, (BLK, BLK), 1)
    return rows >= cols


def softmax_rows(scores):
    top = jnp.max(scores, axis=1, keepdims=True)
    shifted = jnp.exp(scores - top)
    total = jnp.sum(shifted, axis=1, keepdims=True)
    return (shifted * (1.0 / total)).astype(bf16)


def self_fwd_kernel(q_ref, k_ref, v_ref, bias_ref, out_ref, probs_ref):
    mask = causal_mask()
    for head in range(2):
        lanes = slice(head * HD, (head + 1) * HD)
        row = jnp.broadcast_to(bias_ref[0, head : head + 1, :], (BLK, LEN))
        bias = pltpu.roll(row, 0, 1, stride=1, stride_axis=0)
        for block in range(LEN // BLK):
            rows = slice(block * BLK, (block + 1) * BLK)
            wide = (block + 1) * BLK
            scores = dot_t(q_ref[rows, lanes], k_ref[:wide, lanes])
            scores = scores + bias[:, LEN - wide :]
            last = jnp.where(mask, scores[:, wide - BLK :], masked_score)
            if block:
                scores = jnp.concatenate([scores[:, : wide - BLK], last], axis=1)
            else:
                scores = last
            probs = softmax_rows(scores)
            probs_ref[head, rows, :wide] = probs
            out_ref[rows, lanes] = dot(probs, v_ref[:wide, lanes]).astype(bf16)


def cross_fwd_kernel(q_ref, k_ref, v_ref, out_ref, probs_ref):
    for head in range(2):
        lanes = slice(head * HD, (head + 1) * HD)
        probs = softmax_rows(dot_t(q_ref[:, lanes], k_ref[:, lanes]))
        probs_ref[head] = probs
        out_ref[:, lanes] = dot(probs, v_ref[:, lanes]).astype(bf16)


def score_grad_of(probs, weight_grads):
    wide = probs.astype(f32)
    mixed = wide * weight_grads
    inner = jnp.sum(mixed, axis=1, keepdims=True)
    return mixed - wide * inner


def shift_sum(total):
    acc = total[:8]
    for first in range(8, BLK, 8):
        acc = acc + pltpu.roll(total[first : first + 8], LEN - first, 1)
    line = lax.broadcasted_iota(jnp.int32, (8, LEN), 0)
    for bit in (1, 2, 4):
        acc = jnp.where((line & bit) != 0, pltpu.roll(acc, LEN - bit, 1), acc)
    return jnp.sum(acc, axis=0, keepdims=True)


def self_bwd_kernel(q_ref, k_ref, v_ref, g_ref, probs_ref, out_ref, shift_ref, ds_ref):
    for head in range(2):
        lanes = slice(head * HD, (head + 1) * HD)
        total = jnp.zeros((BLK, LEN), f32)
        for block in range(LEN // BLK):
            rows = slice(block * BLK, (block + 1) * BLK)
            wide = (block + 1) * BLK
            weight_grads = dot_t(g_ref[rows, lanes], v_ref[:wide, lanes])
            grads = score_grad_of(probs_ref[head, rows, :wide], weight_grads)
            if wide < LEN:
                total = total + jnp.concatenate([jnp.zeros((BLK, LEN - wide), f32), grads], axis=1)
            else:
                total = total + grads
            short = grads.astype(bf16)
            ds_ref[rows, :wide] = short
            out_ref[0, rows, lanes] = dot(short, k_ref[:wide, lanes]).astype(bf16)
        for block in range(LEN // BLK):
            cols = slice(block * BLK, (block + 1) * BLK)
            rest = slice(block * BLK, LEN)
            out_ref[1, cols, lanes] = t_dot(ds_ref[rest, cols], q_ref[rest, lanes]).astype(bf16)
            out_ref[2, cols, lanes] = t_dot(probs_ref[head, rest, cols], g_ref[rest, lanes]).astype(bf16)
        shift_ref[0, head : head + 1, :] = shift_sum(total)


def cross_bwd_kernel(q_ref, k_ref, v_ref, g_ref, probs_ref, out_ref):
    for head in range(2):
        lanes = slice(head * HD, (head + 1) * HD)
        weight_grads = dot_t(g_ref[:, lanes], v_ref[:, lanes])
        short = score_grad_of(probs_ref[head], weight_grads).astype(bf16)
        out_ref[0, :, lanes] = dot(short, k_ref[:, lanes]).astype(bf16)
        out_ref[1, :, lanes] = t_dot(short, q_ref[:, lanes]).astype(bf16)
        out_ref[2, :, lanes] = t_dot(probs_ref[head], g_ref[:, lanes]).astype(bf16)


def lane_block(first):
    return pl.BlockSpec((LEN, 2 * HD), lambda s, g: (s, first + g))


PROBS = pl.BlockSpec((2, LEN, LEN), lambda s, g: (s * PAIRS + g, 0, 0))
BIAS = pl.BlockSpec((1, 2, LEN), lambda s, g: (g, 0, 0))


def cost(flops, moved):
    return pl.CostEstimate(flops=flops // 16, bytes_accessed=moved // 16, transcendentals=0)


def attention_fwd(queries, query_at, keys, key_at, values, value_at, bias):
    tokens = queries.shape[0]
    sequences = tokens // LEN
    specs = [lane_block(query_at), lane_block(key_at), lane_block(value_at)]
    operands = [queries, keys, values]
    if bias is not None:
        specs.append(BIAS)
        operands.append(bias)
    return pl.pallas_call(
        cross_fwd_kernel if bias is None else self_fwd_kernel,
        grid=(sequences, PAIRS),
        in_specs=specs,
        out_specs=[lane_block(0), PROBS],
        out_shape=[
            jax.ShapeDtypeStruct((tokens, D), bf16),
            jax.ShapeDtypeStruct((sequences * PAIRS * 2, LEN, LEN), bf16),
        ],
        cost_estimate=cost(4 * tokens * LEN * D * 4, tokens * LEN * 24),
    )(*operands)


def attention_bwd(queries, query_at, keys, key_at, values, value_at, grads, probs, causal, first=0, count=PAIRS):
    tokens = queries.shape[0]
    sequences = tokens // LEN
    out_shape = [jax.ShapeDtypeStruct((3, tokens, count * 2 * HD), bf16)]
    out_specs = [pl.BlockSpec((3, LEN, 2 * HD), lambda s, g: (0, s, g))]
    if causal:
        out_shape.append(jax.ShapeDtypeStruct((sequences * count, 2, LEN), f32))
        out_specs.append(pl.BlockSpec((1, 2, LEN), lambda s, g: (s * count + g, 0, 0)))
    return pl.pallas_call(
        self_bwd_kernel if causal else cross_bwd_kernel,
        grid=(sequences, count),
        in_specs=[lane_block(at + first) for at in (query_at, key_at, value_at, 0)]
        + [pl.BlockSpec((2, LEN, LEN), lambda s, g: (s * PAIRS + first + g, 0, 0))],
        out_specs=out_specs,
        out_shape=out_shape,
        scratch_shapes=[pltpu.VMEM((LEN, LEN), bf16)] if causal else [],
        cost_estimate=cost(8 * tokens * LEN * count * 512, tokens * LEN * 4 * count),
    )(queries, keys, values, grads, probs)


def halves(ref, r):
    first = ref[:, pl.ds(pl.multiple_of(r * HALF, 128), HALF)]
    second = ref[:, pl.ds(pl.multiple_of((1 - r) * HALF, 128), HALF)]
    return jnp.concatenate([first, second], axis=1)


def store_halves(ref, r, value):
    ref[:, pl.ds(pl.multiple_of(r * HALF, 128), HALF)] = value[:, :HALF]
    ref[:, pl.ds(pl.multiple_of((1 - r) * HALF, 128), HALF)] = value[:, HALF:]


def rescale_of(values):
    return lax.rsqrt(jnp.mean(values * values, axis=1, keepdims=True) + epsilon)


def norm_back(values, gain, grad):
    rescale = rescale_of(values)
    weighted = gain * grad
    inner = jnp.sum(values * weighted, axis=1, keepdims=True)
    input_grad = rescale * weighted - values * (rescale * rescale * rescale) / D * inner
    return input_grad, jnp.sum(grad * values * rescale, axis=0, keepdims=True)


def tall(low_ref, high_ref):
    return jnp.concatenate([low_ref[...], high_ref[...]], axis=0)


def broad(low_ref, high_ref):
    rows = slice(max(low_ref.shape[0] - HALF, 0), low_ref.shape[0])
    return jnp.concatenate([low_ref[rows, :], high_ref[rows, :]], axis=1)


def stack_kernel(*refs):
    out = refs[-1]
    at = 0
    for ref in refs[:-1]:
        out[at : at + ref.shape[0], :] = ref[...]
        at += ref.shape[0]


def stacked(*parts):
    shape = (sum(p.shape[0] for p in parts), parts[0].shape[1])
    return call(
        stack_kernel, list(parts), [whole(p.shape) for p in parts], shaped(*shape, dtype=bf16), whole(shape)
    )


def by_columns(w00, w10, w01, w11):
    return jnp.concatenate([tall(w00, w10), tall(w01, w11)], axis=1)


def by_rows(w00, w10, w01, w11):
    return jnp.concatenate([broad(w00, w10), broad(w01, w11)], axis=0)


def pre_self_kernel(r_ref, x_ref, gain_ref, w00, w10, w01, w11, n_ref, x32_ref, out_ref):
    @pl.when(pl.program_id(0) == 0)
    def _():
        values = halves(x_ref, r_ref[0]).astype(f32)
        x32_ref[...] = values
        n_ref[...] = (values * rescale_of(values) * gain_ref[...]).astype(bf16)

    out_ref[...] = dot(n_ref[...], by_columns(w00, w10, w01, w11)).astype(bf16)


def encoder_kernel(r_ref, x_ref, w00, w10, w01, w11, x_out_ref, out_ref):
    @pl.when(pl.program_id(0) == 0)
    def _():
        x_out_ref[...] = halves(x_ref, r_ref[0])

    out_ref[...] = dot(x_out_ref[...], by_columns(w00, w10, w01, w11)).astype(bf16)


def join_kernel(base_ref, a_ref, o00, o10, o01, o11, gain_ref, *rest):
    out_ref, n_ref = rest[-3:-1] if len(rest) > 2 else rest
    value = base_ref[...] + dot(a_ref[...], by_rows(o00, o10, o01, o11))
    out_ref[...] = value
    normed = (value * rescale_of(value) * gain_ref[...]).astype(bf16)
    n_ref[...] = normed
    if len(rest) > 2:
        rest[-1][...] = dot(normed, by_columns(*rest[:4])).astype(bf16)


def gelu_parts(v):
    root = 0.7978845608028654
    cubic = 0.044715
    bent = jnp.tanh(root * (v + cubic * (v * v * v)))
    value = 0.5 * v * (1.0 + bent)
    slope = 0.5 * (1.0 + bent) + 0.5 * v * (1.0 - bent * bent) * root * (1.0 + 3.0 * cubic * v * v)
    return value, slope


def ffn_kernel(first, r_ref, n_ref, cot_ref, out_in, ng_in, g0, g1, u0, u1, d0, d1, out_ref, ng_ref, low_ref, dw_ref, nt_ref, lt_ref):
    @pl.when(pl.program_id(0) == 0)
    def _():
        if first:
            low = halves(cot_ref, r_ref[0]).astype(bf16)
            out_ref[...] = out_in[...]
            ng_ref[...] = jnp.zeros_like(ng_ref)
        else:
            low = cot_ref[...]
            out_ref[...] = out_in[...]
            ng_ref[...] = ng_in[...]
        low_ref[...] = low
        nt_ref[...] = n_ref[...].T
        lt_ref[...] = low.T

    normed = n_ref[...]
    gate_w, up_w, down_w = tall(g0, g1), tall(u0, u1), broad(d0, d1)
    gate = dot(normed, gate_w)
    up = dot(normed, up_w)
    hidden_grad = dot_t(low_ref[...], down_w)
    value, slope = gelu_parts(gate)
    hidden = (value * up).astype(bf16)
    gate_grad = (hidden_grad * up * slope).astype(bf16)
    up_grad = (hidden_grad * value).astype(bf16)
    out_ref[...] += dot(hidden, down_w)
    ng_ref[...] += dot_t(gate_grad, gate_w) + dot_t(up_grad, up_w)
    dw_ref[0, 0] = dot(nt_ref[...], gate_grad).astype(bf16)
    dw_ref[1, 0] = dot(nt_ref[...], up_grad).astype(bf16)
    dw_ref[2, 0] = dot(lt_ref[...], hidden).astype(bf16)


def after_ffn_kernel(r_ref, after_ref, cot_ref, ng_ref, gain_ref, o00, o10, o01, o11, grad_ref, low_ref, m_ref, gg_ref):
    third, gain_grad = norm_back(after_ref[...], gain_ref[...], ng_ref[...])
    gg_ref[...] = gain_grad
    total = halves(cot_ref, r_ref[0]) + third
    grad_ref[...] = total
    low = total.astype(bf16)
    low_ref[...] = low
    m_ref[...] = dot_t(low, by_rows(o00, o10, o01, o11)).astype(bf16)


def after_cross_kernel(middle_ref, base_ref, d_ref, q00, q10, q01, q11, gain_ref, o00, o10, o01, o11, grad_ref, low_ref, m_ref, gg_ref):
    normed_grad = dot_t(d_ref[0], by_columns(q00, q10, q01, q11))
    second, gain_grad = norm_back(middle_ref[...], gain_ref[...], normed_grad)
    gg_ref[...] = gain_grad
    total = base_ref[...] + second
    grad_ref[...] = total
    low = total.astype(bf16)
    low_ref[...] = low
    m_ref[...] = dot_t(low, by_rows(o00, o10, o01, o11)).astype(bf16)


def cross_grads_kernel(enc_ref, n_ref, low_ref, mid_ref, d_ref, att_ref, self_ref, own_ref, other_ref):
    turned = enc_ref[...].T
    pairs = (
        (turned, d_ref[1]),
        (turned, d_ref[2]),
        (n_ref[...].T, d_ref[0]),
        (low_ref[...].T, att_ref[...]),
        (mid_ref[...].T, self_ref[...]),
    )
    for place, (left, right) in enumerate(pairs):
        grad = dot(left, right).astype(bf16)
        own_ref[place] = grad[:, :HALF]
        other_ref[place] = grad[:, HALF:]


def self_grads_kernel(n_ref, d_ref, out_ref, nt_ref):
    @pl.when(pl.program_id(0) == 0)
    def _():
        nt_ref[...] = n_ref[...].T

    out_ref[0] = dot(nt_ref[...], d_ref[0]).astype(bf16)


def input_grad_kernel(r_ref, x_ref, base_ref, gain_ref, d0_ref, d1_ref, w00, w10, w01, w11, out_ref, gg_ref, acc_ref):
    j = pl.program_id(0)
    part = dot_t(d0_ref[0], tall(w00, w10)) + dot_t(d1_ref[0], tall(w01, w11))

    @pl.when(j == 0)
    def _():
        acc_ref[...] = part

    @pl.when(j != 0)
    def _():
        acc_ref[...] += part

    @pl.when(j == 2)
    def _():
        first, gain_grad = norm_back(x_ref[...], gain_ref[...], acc_ref[...])
        gg_ref[...] = gain_grad
        store_halves(out_ref, r_ref[0], base_ref[...] + first)


def encoder_grad_kernel(r_ref, out_in, d_ref, w00, w10, w01, w11, out_ref, layer_ref, acc_ref):
    j = pl.program_id(0)
    part = dot_t(d_ref[0], by_columns(w00, w10, w01, w11))

    @pl.when(j == 0)
    def _():
        acc_ref[...] = part
        store_halves(layer_ref, r_ref[0], out_in[...])

    @pl.when(j == 1)
    def _():
        store_halves(out_ref, r_ref[0], acc_ref[...] + part)


SCALAR = pl.BlockSpec(memory_space=pltpu.SMEM)


def whole(shape):
    return pl.BlockSpec(shape, lambda *grid: (0,) * len(shape))


def square(row):
    return pl.BlockSpec((HALF, HALF), lambda *grid: (row, 0))


def moving(first):
    return pl.BlockSpec((HALF, HALF), lambda j: (first + j, 0))


def shaped(*shape, dtype=f32):
    return jax.ShapeDtypeStruct(shape, dtype)


def call(kernel, operands, in_specs, out_shape, out_specs, grid=(1,), scratch=(), flops=0):
    moved = sum(x.size * x.dtype.itemsize for x in operands)
    return pl.pallas_call(
        kernel,
        grid=grid,
        in_specs=in_specs,
        out_specs=out_specs,
        out_shape=out_shape,
        scratch_shapes=list(scratch),
        cost_estimate=cost(flops, moved),
        compiler_params=pltpu.CompilerParams(vmem_limit_bytes=56 << 20),
    )(*operands)


def added(a, b):
    return (a.astype(f32) + b.astype(f32)).astype(bf16)


def side_of(bit):
    return lax.bitwise_and(lax.div(lax.axis_index("dp"), jnp.int32(bit)), jnp.int32(1))


def chosen(side, low, high):
    return jnp.where(side == 0, low, high), jnp.where(side == 0, high, low)


QUARTER = HALF // 2


def over_dp(bit, x):
    count = lax.axis_size("dp")
    return lax.ppermute(x, "dp", [(i, i ^ bit) for i in range(count)])


def row_first(own, came):
    total = added(own, came)
    keep, send = pin(total[:, :HALF], total[:, HALF:])
    (came,) = yield (over_row(send),)
    total = added(keep, came)
    keep, send = chosen(side_of(1), total[:, :QUARTER], total[:, QUARTER:])
    (came,) = yield (over_dp(1, send),)
    yield added(keep, came)


def dp_first(own, came):
    total = added(own, came)
    total = total.reshape(total.shape[0], 2, 2, QUARTER, total.shape[2])
    keep, send = pin(*chosen(side_of(1), total[:, :, 0], total[:, :, 1]))
    (came,) = yield (over_dp(1, send),)
    total = added(keep, came)
    (came,) = yield (over_row(total[:, 1]),)
    yield added(total[:, 0], came)


def beyond(dp_count, block):
    undo = [1]
    bit = 2
    while bit < dp_count:
        rows = block.shape[1]
        if rows % 32 == 0:
            block, send = chosen(side_of(bit), block[:, : rows // 2], block[:, rows // 2 :])
            undo.append(bit)
        else:
            send = block
        (came,) = yield (over_dp(bit, send),)
        block = added(block, came)
        bit *= 2
    for bit in reversed(undo):
        (came,) = yield (over_dp(bit, block),)
        first, second = chosen(side_of(bit), block, came)
        block = jnp.concatenate([first, second], axis=1)
    yield block.astype(f32)


def small_sum(dp_count, small):
    (came,) = yield (over_col(small[:, 1]),)
    small = small[:, 0] + came
    (came,) = yield (over_row(small[1]),)
    small = small[0] + came
    bits = [1 << i for i in range(dp_count.bit_length() - 1)]
    for bit in bits[1:] + bits[:1]:
        (came,) = yield (over_dp(bit, small),)
        small = small + came
    yield small


def row_reduction(dp_count, own, came):
    a = row_first(own, came)
    came = yield next(a)
    came = yield a.send(came)
    yield from beyond(dp_count, a.send(came))


def whole_reduction(dp_count, left, right):
    a, b = row_first(*left), dp_first(*right)
    came = yield next(a) + next(b)
    came = yield a.send(came[:1]) + b.send(came[1:])
    block = jnp.concatenate([a.send(came[:1]), b.send(came[1:])], axis=0)
    yield from beyond(dp_count, block)


def local(
    layer_input,
    encoder_states,
    cotangent,
    buckets,
    gain_self,
    gain_cross,
    gain_ffn,
    self_query,
    self_key,
    self_value,
    self_out,
    cross_query,
    cross_key,
    cross_value,
    cross_out,
    ffn_gate,
    ffn_up,
    ffn_down,
    rel_table,
    dp_count,
):
    r = lax.axis_index("row")
    c = lax.axis_index("col")
    own_small = jnp.concatenate([gain_self, gain_cross, gain_ffn, rel_table.reshape(-1)])
    quarter = gain_self.shape[0]
    onehot = (buckets[:, None] == jnp.arange(NB, dtype=jnp.int32)[None, :]).astype(f32)
    placed = jnp.roll(onehot[::-1], LEN - BLK + 1, axis=0)
    tokens = layer_input.shape[0]
    row_index = jnp.reshape(r, (1,))
    both = range(2)
    tok = whole((tokens, D))
    tok_half = whole((tokens, HALF))
    vec = whole((1, D))
    tok_f32, tok_bf16 = shaped(tokens, D), shaped(tokens, D, dtype=bf16)
    half_bf16 = shaped(tokens, HALF, dtype=bf16)
    dense = 2 * tokens * D * HALF

    tokens = layer_input.shape[0]
    row_index = jnp.reshape(r, (1,))
    tok = whole((tokens, D))
    vec = whole((1, D))
    tok_f32, tok_bf16 = shaped(tokens, D), shaped(tokens, D, dtype=bf16)
    dense = 2 * tokens * D * D
    column = pl.BlockSpec((tokens, D), lambda j: (0, j))

    def gathered(own, arrived):
        return [own, arrived, over_col(own), over_col(arrived)]

    width = ffn_gate.shape[1]
    part = width // 2
    small_row = over_row(own_small)
    msg_self = stacked(self_query, self_key, self_value)
    msg_self, small_row, rest_weights = pin(
        msg_self,
        small_row,
        (self_out, cross_query, cross_key, cross_value, ffn_down, cross_out, ffn_gate, ffn_up),
    )
    got_self = over_row(msg_self)
    msg_mid = stacked(*rest_weights[:4])
    msg_down = stacked(*rest_weights[4:6])
    msg_up = stacked(*rest_weights[6:])
    small_row, msg_mid, msg_up, msg_down = pin(small_row, msg_mid, msg_up, msg_down)
    by_row = jnp.stack([own_small, small_row], axis=0)
    by_both = jnp.stack([by_row, over_col(by_row)], axis=1)
    by_col = local_order(by_both, c, 1)
    gains = [by_col[:, :, i * quarter : (i + 1) * quarter].reshape(1, D) for i in range(3)]
    tables = local_order(by_both, r, 0)[:, :, 3 * quarter :].transpose(1, 0, 2)
    bias_rows = lax.dot_general(
        tables.reshape(12, NB), placed, (((1,), (1,)), ((), ())), precision=lax.Precision.HIGHEST
    ).reshape(PAIRS, 2, LEN)

    w_self = gathered(msg_self, got_self)
    msg_mid, got_self, bias_rows = pin(msg_mid, got_self, bias_rows)
    got_mid = over_row(msg_mid)
    so, cqw, ckw, cvw = range(4)
    normed_one, x, qkv = call(
        pre_self_kernel,
        [row_index, layer_input, gains[0]] + w_self,
        [SCALAR, tok, vec] + [moving(0)] * 4,
        [tok_bf16, tok_f32, shaped(tokens, 3 * D, dtype=bf16)],
        [tok, tok, column],
        grid=(3,),
        flops=3 * dense,
    )
    self_att, self_probs = attention_fwd(qkv, 0, qkv, PAIRS, qkv, 2 * PAIRS, bias_rows)
    self_att, got_mid, msg_up, msg_down = pin(self_att, got_mid, msg_up, msg_down)
    w_mid = gathered(msg_mid, got_mid)
    got_down, got_up = over_row(msg_down), over_row(msg_up)
    encoder, kv = call(
        encoder_kernel,
        [row_index, encoder_states] + w_mid,
        [SCALAR, tok] + [moving(ckw)] * 4,
        [tok_bf16, shaped(tokens, 2 * D, dtype=bf16)],
        [tok, column],
        grid=(2,),
        flops=2 * dense,
    )
    middle, normed_two, cq = call(
        join_kernel,
        [x, self_att] + w_mid + [gains[1]] + w_mid,
        [tok, tok] + [square(so)] * 4 + [vec] + [square(cqw)] * 4,
        [tok_f32, tok_bf16, tok_bf16],
        [tok, tok, tok],
        flops=2 * dense,
    )
    cross_att, cross_probs = attention_fwd(cq, 0, kv, 0, kv, PAIRS, None)
    cross_att, got_down = pin(cross_att, got_down)
    w_down = gathered(msg_down, got_down)
    after, normed_three = call(
        join_kernel,
        [middle, cross_att] + w_down + [gains[2]],
        [tok, tok] + [whole(msg_down.shape)] * 4 + [vec],
        [tok_f32, tok_bf16],
        [tok, tok],
        flops=dense,
    )

    normed_three, got_up = pin(normed_three, got_up)
    w_up = gathered(msg_up, got_up)
    tile = 256
    per = part // tile
    layer_local, ng, out_low = after, after, cotangent
    ffn_grads = [None, None]
    for h in (1, 0):
        up, down = w_up[2 * h : 2 * h + 2], w_down[2 * h : 2 * h + 2]
        layer_local, ng, out_low, ffn_grads[h] = call(
            functools.partial(ffn_kernel, h == 1),
            [row_index, normed_three, out_low, layer_local, ng] + up + up + down,
            [SCALAR]
            + [tok] * 4
            + [pl.BlockSpec((HALF, tile), lambda t: (0, t))] * 2
            + [pl.BlockSpec((HALF, tile), lambda t: (1, t))] * 2
            + [pl.BlockSpec((tile, HALF), lambda t: (t, 0))] * 2,
            [tok_f32, tok_f32, tok_bf16, shaped(3, 2, D, part, dtype=bf16)],
            [tok] * 3 + [pl.BlockSpec((3, 1, D, tile), lambda t: (0, t // per, 0, t % per))],
            grid=(width // tile,),
            scratch=[pltpu.VMEM((D, tokens), bf16)] * 2,
            flops=9 * 2 * tokens * D * width,
        )
        if h == 1:
            came = over_col(ffn_grads[1])
    out_low, ffn_grads[0], came, ng = pin(out_low, ffn_grads[0], came, ng)
    ffn_a = row_first(ffn_grads[0][:, 0], came[:, 0])
    ffn_b = dp_first(ffn_grads[0][:, 1], came[:, 1])
    came_a, came_b = next(ffn_a), next(ffn_b)
    after_grad, after_low, cross_mixed, gain_ffn_grad = call(
        after_ffn_kernel,
        [row_index, after, cotangent, ng, gains[2]] + w_down,
        [SCALAR, tok, tok, tok, vec] + [whole(msg_down.shape)] * 4,
        [tok_f32, tok_bf16, tok_bf16, shaped(1, D)],
        [tok, tok, tok, vec],
        flops=dense,
    )
    (cross_back,) = attention_bwd(cq, 0, kv, 0, kv, PAIRS, cross_mixed, cross_probs, False)
    cross_back, came_a, came_b = pin(cross_back, came_a, came_b)
    came_a, came_b = ffn_a.send(came_a), ffn_b.send(came_b)
    middle_grad, middle_low, self_mixed, gain_cross_grad = call(
        after_cross_kernel,
        [middle, after_grad, cross_back] + w_mid + [gains[1]] + w_mid,
        [tok, tok, pl.BlockSpec((1, tokens, D), lambda j: (0, 0, 0))]
        + [square(cqw)] * 4
        + [vec]
        + [square(so)] * 4,
        [tok_f32, tok_bf16, tok_bf16, shaped(1, D)],
        [tok, tok, tok, vec],
        flops=2 * dense,
    )
    pieces = shaped(5, D, HALF, dtype=bf16)
    cross_own, cross_other = call(
        cross_grads_kernel,
        [encoder, normed_two, after_low, middle_low, cross_back, cross_att, self_att],
        [tok] * 4 + [whole((3, tokens, D))] + [tok] * 2,
        [pieces, pieces],
        [whole((5, D, HALF))] * 2,
        flops=5 * dense,
    )
    self_mixed, cross_other, came_a, came_b = pin(self_mixed, cross_other, came_a, came_b)
    ffn = beyond(dp_count, jnp.concatenate([ffn_a.send(came_a), ffn_b.send(came_b)], axis=0))
    ffn_came = next(ffn)
    cross_came = over_col(cross_other)

    self_back, shifts, self_grads = [None, None], [None, None], [None, None]

    def self_half(h):
        back, shift = attention_bwd(
            qkv, 0, qkv, PAIRS, qkv, 2 * PAIRS, self_mixed, self_probs, True, h * PAIRS // 2, PAIRS // 2
        )
        return back, shift

    def self_half_grads(back):
        return call(
            self_grads_kernel,
            [normed_one, back],
            [tok, pl.BlockSpec((1, tokens, HALF), lambda j: (j, 0, 0))],
            shaped(3, D, HALF, dtype=bf16),
            pl.BlockSpec((1, D, HALF), lambda j: (j, 0, 0)),
            grid=(3,),
            scratch=[pltpu.VMEM((D, tokens), bf16)],
            flops=3 * dense // 2,
        )

    self_back[1], shifts[1] = self_half(1)
    self_back[1], self_mixed, cross_came, ffn_came = pin(
        self_back[1], self_mixed, cross_came, ffn_came
    )
    cross = whole_reduction(
        dp_count, (cross_own[:3], cross_came[:3]), (cross_own[3:], cross_came[3:])
    )
    cross_came = next(cross)
    ffn_came = ffn.send(ffn_came)
    self_grads[1] = self_half_grads(self_back[1])
    self_mixed, self_grads[1] = pin(self_mixed, self_grads[1])
    self_came = over_col(self_grads[1])
    self_back[0], shifts[0] = self_half(0)
    self_back[0], ffn_came = pin(self_back[0], ffn_came)
    ffn_came = ffn.send(ffn_came)
    self_grads[0] = self_half_grads(self_back[0])
    self_grads[0], self_came, cross_came, middle_grad, layer_local = pin(
        self_grads[0], self_came, cross_came, middle_grad, layer_local
    )
    own = row_reduction(dp_count, self_grads[0], self_came)
    self_came = next(own)
    cross_came = cross.send(cross_came)
    encoder_grad, layer_output = call(
        encoder_grad_kernel,
        [row_index, layer_local, cross_back] + w_mid,
        [SCALAR, tok, pl.BlockSpec((1, tokens, D), lambda j: (1 + j, 0, 0))] + [moving(ckw)] * 4,
        [tok_f32, tok_f32],
        [tok, tok],
        grid=(2,),
        scratch=[pltpu.VMEM((tokens, D), f32)],
        flops=2 * dense,
    )
    cross_came, ffn_came, middle_grad, layer_output = pin(
        cross_came, ffn_came, middle_grad, layer_output
    )
    cross_came = cross.send(cross_came)
    ffn_came = ffn.send(ffn_came)
    one = pl.BlockSpec((1, tokens, HALF), lambda j: (j, 0, 0))
    input_grad, gain_self_grad = call(
        input_grad_kernel,
        [row_index, x, middle_grad, gains[0], self_back[0], self_back[1]] + w_self,
        [SCALAR, tok, tok, vec, one, one] + [moving(0)] * 4,
        [tok_f32, shaped(1, D)],
        [tok, vec],
        grid=(3,),
        scratch=[pltpu.VMEM((tokens, D), f32)],
        flops=3 * dense,
    )
    shift_sums = jnp.concatenate(
        [jnp.sum(part_sums.reshape(-1, PAIRS, LEN), axis=0) for part_sums in shifts], axis=0
    )
    table_local = jnp.dot(
        shift_sums, placed, precision=lax.Precision.HIGHEST
    ).reshape(2, 2, 3 * NB)
    table_local = local_order(table_local, r, 1).transpose(1, 0, 2)
    gains_local = jnp.stack([gain_self_grad, gain_cross_grad, gain_ffn_grad], axis=0)
    gains_local = local_order(gains_local.reshape(3, 2, 2, quarter), c, 2)
    gains_local = gains_local.transpose(1, 2, 0, 3).reshape(2, 2, 3 * quarter)
    small = jnp.concatenate([gains_local, table_local], axis=2)
    groups = [own, cross, ffn, small_sum(dp_count, small)]
    under_way = [self_came, cross_came, ffn_came, None]
    small, under_way[0], under_way[1], under_way[2] = pin(small, *under_way[:3])
    sums = [None] * 4
    while any(total is None for total in sums):
        live = [i for i in range(4) if sums[i] is None]
        if len(live) > 1 and under_way[2] is not None and under_way[2][0].shape[1] == QUARTER:
            live = [i for i in live if i != 2]
        arrived = _pinned([under_way[i] for i in live])
        for i, came in zip(live, arrived):
            started = next(groups[i]) if came is None else groups[i].send(came)
            if isinstance(started, tuple):
                under_way[i] = started
            else:
                sums[i] = started
    self_sum, cross_sum, ffn_sum, small = sums
    gains_own = small[: 3 * quarter].reshape(3, quarter)
    table_own = small[3 * quarter :].reshape(1, 1, 3, NB)

    ffn_sum = ffn_sum.reshape(2, 3, HALF, part)
    gate_sum, up_sum = (
        jnp.concatenate([ffn_sum[0, k], ffn_sum[1, k]], axis=1) for k in range(2)
    )
    down_sum = jnp.concatenate([ffn_sum[0, 2].T, ffn_sum[1, 2].T], axis=0)
    return (
        layer_output,
        input_grad,
        encoder_grad,
        gains_own[0],
        gains_own[1],
        gains_own[2],
        self_sum[0],
        self_sum[1],
        self_sum[2],
        cross_sum[4].T,
        cross_sum[2],
        cross_sum[0],
        cross_sum[1],
        cross_sum[3].T,
        gate_sum,
        up_sum,
        down_sum,
        table_own,
    )


def solution(mesh):
    tokens = P(("dp", "row", "col"), None)
    gain = P(("row", "col"))
    columns = P("row", "col")
    rows = P("col", "row")
    table = P("col", "row", None, None)
    weights = (columns,) * 3 + (rows,) + (columns,) * 3 + (rows,) + (columns,) * 2 + (rows,)
    in_specs = (tokens,) * 3 + (P(),) + (gain,) * 3 + weights + (table,)
    out_specs = (tokens,) * 3 + (gain,) * 3 + weights + (table,)
    body = functools.partial(local, dp_count=mesh.shape["dp"])
    return jax.shard_map(
        body, mesh=mesh, in_specs=in_specs, out_specs=out_specs, check_vma=False
    )
```

```python
import functools

import jax
import jax.numpy as jnp
from jax import lax
from jax.experimental import pallas as pl
from jax.experimental.pallas import tpu as pltpu
from jax.sharding import PartitionSpec as P

D = 768
HD = 64
NB = 32
LEN = 512
BLK = 256
HALF = D // 2
PAIRS = D // (2 * HD)

epsilon = 1e-06
masked_score = -1e30
f32 = jnp.float32
bf16 = jnp.bfloat16
SWAP = [(0, 1), (1, 0)]


def over_row(x):
    return lax.ppermute(x, "row", SWAP)


def over_col(x):
    return lax.ppermute(x, "col", SWAP)


def dot(a, b):
    return jnp.dot(a, b, preferred_element_type=f32)


def dot_t(a, b):
    return lax.dot_general(a, b, (((1,), (1,)), ((), ())), preferred_element_type=f32)


def t_dot(a, b):
    return lax.dot_general(a, b, (((0,), (0,)), ((), ())), preferred_element_type=f32)


def pin(*values):
    return lax.optimization_barrier(values)


def _pinned(values):
    present = [v for v in values if v is not None]
    held = list(pin(*present))
    return [None if v is None else held.pop(0) for v in values]


def local_order(x, flag, axis):
    first, second = jnp.split(x, 2, axis=axis)
    swapped = jnp.concatenate([second, first], axis=axis)
    return jnp.where(flag == 0, x, swapped)


def causal_mask():
    rows = lax.broadcasted_iota(jnp.int32, (BLK, BLK), 0)
    cols = lax.broadcasted_iota(jnp.int32, (BLK, BLK), 1)
    return rows >= cols


def softmax_rows(scores):
    top = jnp.max(scores, axis=1, keepdims=True)
    shifted = jnp.exp(scores - top)
    total = jnp.sum(shifted, axis=1, keepdims=True)
    return (shifted * (1.0 / total)).astype(bf16)


def self_fwd_kernel(q_ref, k_ref, v_ref, bias_ref, out_ref, probs_ref):
    mask = causal_mask()
    for head in range(2):
        lanes = slice(head * HD, (head + 1) * HD)
        row = jnp.broadcast_to(bias_ref[0, head : head + 1, :], (BLK, LEN))
        bias = pltpu.roll(row, 0, 1, stride=1, stride_axis=0)
        for block in range(LEN // BLK):
            rows = slice(block * BLK, (block + 1) * BLK)
            wide = (block + 1) * BLK
            scores = dot_t(q_ref[rows, lanes], k_ref[:wide, lanes])
            scores = scores + bias[:, LEN - wide :]
            last = jnp.where(mask, scores[:, wide - BLK :], masked_score)
            if block:
                scores = jnp.concatenate([scores[:, : wide - BLK], last], axis=1)
            else:
                scores = last
            probs = softmax_rows(scores)
            probs_ref[head, rows, :wide] = probs
            out_ref[rows, lanes] = dot(probs, v_ref[:wide, lanes]).astype(bf16)


def cross_fwd_kernel(q_ref, k_ref, v_ref, out_ref, probs_ref):
    for head in range(2):
        lanes = slice(head * HD, (head + 1) * HD)
        probs = softmax_rows(dot_t(q_ref[:, lanes], k_ref[:, lanes]))
        probs_ref[head] = probs
        out_ref[:, lanes] = dot(probs, v_ref[:, lanes]).astype(bf16)


def score_grad_of(probs, weight_grads):
    wide = probs.astype(f32)
    mixed = wide * weight_grads
    inner = jnp.sum(mixed, axis=1, keepdims=True)
    return mixed - wide * inner


def shift_sum(total):
    acc = total[:8]
    for first in range(8, BLK, 8):
        acc = acc + pltpu.roll(total[first : first + 8], LEN - first, 1)
    line = lax.broadcasted_iota(jnp.int32, (8, LEN), 0)
    for bit in (1, 2, 4):
        acc = jnp.where((line & bit) != 0, pltpu.roll(acc, LEN - bit, 1), acc)
    return jnp.sum(acc, axis=0, keepdims=True)


def self_bwd_kernel(q_ref, k_ref, v_ref, g_ref, probs_ref, out_ref, shift_ref, ds_ref):
    for head in range(2):
        lanes = slice(head * HD, (head + 1) * HD)
        total = jnp.zeros((BLK, LEN), f32)
        for block in range(LEN // BLK):
            rows = slice(block * BLK, (block + 1) * BLK)
            wide = (block + 1) * BLK
            weight_grads = dot_t(g_ref[rows, lanes], v_ref[:wide, lanes])
            grads = score_grad_of(probs_ref[head, rows, :wide], weight_grads)
            if wide < LEN:
                total = total + jnp.concatenate([jnp.zeros((BLK, LEN - wide), f32), grads], axis=1)
            else:
                total = total + grads
            short = grads.astype(bf16)
            ds_ref[rows, :wide] = short
            out_ref[0, rows, lanes] = dot(short, k_ref[:wide, lanes]).astype(bf16)
        for block in range(LEN // BLK):
            cols = slice(block * BLK, (block + 1) * BLK)
            rest = slice(block * BLK, LEN)
            out_ref[1, cols, lanes] = t_dot(ds_ref[rest, cols], q_ref[rest, lanes]).astype(bf16)
            out_ref[2, cols, lanes] = t_dot(probs_ref[head, rest, cols], g_ref[rest, lanes]).astype(bf16)
        shift_ref[0, head : head + 1, :] = shift_sum(total)


def cross_bwd_kernel(q_ref, k_ref, v_ref, g_ref, probs_ref, out_ref):
    for head in range(2):
        lanes = slice(head * HD, (head + 1) * HD)
        weight_grads = dot_t(g_ref[:, lanes], v_ref[:, lanes])
        short = score_grad_of(probs_ref[head], weight_grads).astype(bf16)
        out_ref[0, :, lanes] = dot(short, k_ref[:, lanes]).astype(bf16)
        out_ref[1, :, lanes] = t_dot(short, q_ref[:, lanes]).astype(bf16)
        out_ref[2, :, lanes] = t_dot(probs_ref[head], g_ref[:, lanes]).astype(bf16)


def lane_block(first):
    return pl.BlockSpec((LEN, 2 * HD), lambda s, g: (s, first + g))


PROBS = pl.BlockSpec((2, LEN, LEN), lambda s, g: (s * PAIRS + g, 0, 0))
BIAS = pl.BlockSpec((1, 2, LEN), lambda s, g: (g, 0, 0))


def cost(flops, moved):
    return pl.CostEstimate(flops=flops // 16, bytes_accessed=moved // 16, transcendentals=0)


def attention_fwd(queries, query_at, keys, key_at, values, value_at, bias):
    tokens = queries.shape[0]
    sequences = tokens // LEN
    specs = [lane_block(query_at), lane_block(key_at), lane_block(value_at)]
    operands = [queries, keys, values]
    if bias is not None:
        specs.append(BIAS)
        operands.append(bias)
    return pl.pallas_call(
        cross_fwd_kernel if bias is None else self_fwd_kernel,
        grid=(sequences, PAIRS),
        in_specs=specs,
        out_specs=[lane_block(0), PROBS],
        out_shape=[
            jax.ShapeDtypeStruct((tokens, D), bf16),
            jax.ShapeDtypeStruct((sequences * PAIRS * 2, LEN, LEN), bf16),
        ],
        cost_estimate=cost(4 * tokens * LEN * D * 4, tokens * LEN * 24),
    )(*operands)


def attention_bwd(queries, query_at, keys, key_at, values, value_at, grads, probs, causal, first=0, count=PAIRS):
    tokens = queries.shape[0]
    sequences = tokens // LEN
    out_shape = [jax.ShapeDtypeStruct((3, tokens, count * 2 * HD), bf16)]
    out_specs = [pl.BlockSpec((3, LEN, 2 * HD), lambda s, g: (0, s, g))]
    if causal:
        out_shape.append(jax.ShapeDtypeStruct((sequences * count, 2, LEN), f32))
        out_specs.append(pl.BlockSpec((1, 2, LEN), lambda s, g: (s * count + g, 0, 0)))
    return pl.pallas_call(
        self_bwd_kernel if causal else cross_bwd_kernel,
        grid=(sequences, count),
        in_specs=[lane_block(at + first) for at in (query_at, key_at, value_at, 0)]
        + [pl.BlockSpec((2, LEN, LEN), lambda s, g: (s * PAIRS + first + g, 0, 0))],
        out_specs=out_specs,
        out_shape=out_shape,
        scratch_shapes=[pltpu.VMEM((LEN, LEN), bf16)] if causal else [],
        cost_estimate=cost(8 * tokens * LEN * count * 512, tokens * LEN * 4 * count),
    )(queries, keys, values, grads, probs)


def halves(ref, r):
    first = ref[:, pl.ds(pl.multiple_of(r * HALF, 128), HALF)]
    second = ref[:, pl.ds(pl.multiple_of((1 - r) * HALF, 128), HALF)]
    return jnp.concatenate([first, second], axis=1)


def store_halves(ref, r, value):
    ref[:, pl.ds(pl.multiple_of(r * HALF, 128), HALF)] = value[:, :HALF]
    ref[:, pl.ds(pl.multiple_of((1 - r) * HALF, 128), HALF)] = value[:, HALF:]


def rescale_of(values):
    return lax.rsqrt(jnp.mean(values * values, axis=1, keepdims=True) + epsilon)


def norm_back(values, gain, grad):
    rescale = rescale_of(values)
    weighted = gain * grad
    inner = jnp.sum(values * weighted, axis=1, keepdims=True)
    input_grad = rescale * weighted - values * (rescale * rescale * rescale) / D * inner
    return input_grad, jnp.sum(grad * values * rescale, axis=0, keepdims=True)


def tall(low_ref, high_ref):
    return jnp.concatenate([low_ref[...], high_ref[...]], axis=0)


def broad(low_ref, high_ref):
    rows = slice(max(low_ref.shape[0] - HALF, 0), low_ref.shape[0])
    return jnp.concatenate([low_ref[rows, :], high_ref[rows, :]], axis=1)


def stack_kernel(*refs):
    out = refs[-1]
    at = 0
    for ref in refs[:-1]:
        out[at : at + ref.shape[0], :] = ref[...]
        at += ref.shape[0]


def stacked(*parts):
    shape = (sum(p.shape[0] for p in parts), parts[0].shape[1])
    return call(
        stack_kernel, list(parts), [whole(p.shape) for p in parts], shaped(*shape, dtype=bf16), whole(shape)
    )


def by_columns(w00, w10, w01, w11):
    return jnp.concatenate([tall(w00, w10), tall(w01, w11)], axis=1)


def by_rows(w00, w10, w01, w11):
    return jnp.concatenate([broad(w00, w10), broad(w01, w11)], axis=0)


def pre_self_kernel(r_ref, x_ref, gain_ref, w00, w10, w01, w11, n_ref, x32_ref, out_ref):
    @pl.when(pl.program_id(0) == 0)
    def _():
        values = halves(x_ref, r_ref[0]).astype(f32)
        x32_ref[...] = values
        n_ref[...] = (values * rescale_of(values) * gain_ref[...]).astype(bf16)

    out_ref[...] = dot(n_ref[...], by_columns(w00, w10, w01, w11)).astype(bf16)


def encoder_kernel(r_ref, x_ref, w00, w10, w01, w11, x_out_ref, out_ref):
    @pl.when(pl.program_id(0) == 0)
    def _():
        x_out_ref[...] = halves(x_ref, r_ref[0])

    out_ref[...] = dot(x_out_ref[...], by_columns(w00, w10, w01, w11)).astype(bf16)


def join_kernel(base_ref, a_ref, o00, o10, o01, o11, gain_ref, *rest):
    out_ref, n_ref = rest[-3:-1] if len(rest) > 2 else rest
    value = base_ref[...] + dot(a_ref[...], by_rows(o00, o10, o01, o11))
    out_ref[...] = value
    normed = (value * rescale_of(value) * gain_ref[...]).astype(bf16)
    n_ref[...] = normed
    if len(rest) > 2:
        rest[-1][...] = dot(normed, by_columns(*rest[:4])).astype(bf16)


def gelu_parts(v):
    root = 0.7978845608028654
    cubic = 0.044715
    bent = jnp.tanh(root * (v + cubic * (v * v * v)))
    value = 0.5 * v * (1.0 + bent)
    slope = 0.5 * (1.0 + bent) + 0.5 * v * (1.0 - bent * bent) * root * (1.0 + 3.0 * cubic * v * v)
    return value, slope


def ffn_kernel(first, r_ref, n_ref, cot_ref, out_in, ng_in, g0, g1, u0, u1, d0, d1, out_ref, ng_ref, low_ref, dw_ref, nt_ref, lt_ref):
    @pl.when(pl.program_id(0) == 0)
    def _():
        if first:
            low = halves(cot_ref, r_ref[0]).astype(bf16)
            out_ref[...] = out_in[...]
            ng_ref[...] = jnp.zeros_like(ng_ref)
        else:
            low = cot_ref[...]
            out_ref[...] = out_in[...]
            ng_ref[...] = ng_in[...]
        low_ref[...] = low
        nt_ref[...] = n_ref[...].T
        lt_ref[...] = low.T

    normed = n_ref[...]
    gate_w, up_w, down_w = tall(g0, g1), tall(u0, u1), jnp.concatenate([d0[...], d1[...]], axis=1)
    gate = dot(normed, gate_w)
    up = dot(normed, up_w)
    hidden_grad = dot_t(low_ref[...], down_w)
    value, slope = gelu_parts(gate)
    hidden = (value * up).astype(bf16)
    gate_grad = (hidden_grad * up * slope).astype(bf16)
    up_grad = (hidden_grad * value).astype(bf16)
    out_ref[...] += dot(hidden, down_w)
    ng_ref[...] += dot_t(gate_grad, gate_w) + dot_t(up_grad, up_w)
    dw_ref[0, 0] = dot(nt_ref[...], gate_grad).astype(bf16)
    dw_ref[1, 0] = dot(nt_ref[...], up_grad).astype(bf16)
    dw_ref[2, 0] = dot(lt_ref[...], hidden).astype(bf16)


def after_ffn_kernel(r_ref, after_ref, cot_ref, ng_ref, gain_ref, o00, o10, o01, o11, grad_ref, low_ref, m_ref, gg_ref):
    third, gain_grad = norm_back(after_ref[...], gain_ref[...], ng_ref[...])
    gg_ref[...] = gain_grad
    total = halves(cot_ref, r_ref[0]) + third
    grad_ref[...] = total
    low = total.astype(bf16)
    low_ref[...] = low
    m_ref[...] = dot_t(low, by_rows(o00, o10, o01, o11)).astype(bf16)


def after_cross_kernel(middle_ref, base_ref, d_ref, q00, q10, q01, q11, gain_ref, o00, o10, o01, o11, grad_ref, low_ref, m_ref, gg_ref):
    normed_grad = dot_t(d_ref[0], by_columns(q00, q10, q01, q11))
    second, gain_grad = norm_back(middle_ref[...], gain_ref[...], normed_grad)
    gg_ref[...] = gain_grad
    total = base_ref[...] + second
    grad_ref[...] = total
    low = total.astype(bf16)
    low_ref[...] = low
    m_ref[...] = dot_t(low, by_rows(o00, o10, o01, o11)).astype(bf16)


def cross_grads_kernel(enc_ref, n_ref, low_ref, mid_ref, d_ref, att_ref, self_ref, own_ref, other_ref):
    turned = enc_ref[...].T
    pairs = (
        (turned, d_ref[1]),
        (turned, d_ref[2]),
        (n_ref[...].T, d_ref[0]),
        (low_ref[...].T, att_ref[...]),
        (mid_ref[...].T, self_ref[...]),
    )
    for place, (left, right) in enumerate(pairs):
        grad = dot(left, right).astype(bf16)
        own_ref[place] = grad[:, :HALF]
        other_ref[place] = grad[:, HALF:]


def self_grads_kernel(n_ref, d_ref, out_ref, nt_ref):
    @pl.when(pl.program_id(0) == 0)
    def _():
        nt_ref[...] = n_ref[...].T

    out_ref[0] = dot(nt_ref[...], d_ref[0]).astype(bf16)


def input_grad_kernel(r_ref, x_ref, base_ref, gain_ref, d0_ref, d1_ref, w00, w10, w01, w11, out_ref, gg_ref, acc_ref):
    j = pl.program_id(0)
    part = dot_t(d0_ref[0], tall(w00, w10)) + dot_t(d1_ref[0], tall(w01, w11))

    @pl.when(j == 0)
    def _():
        acc_ref[...] = part

    @pl.when(j != 0)
    def _():
        acc_ref[...] += part

    @pl.when(j == 2)
    def _():
        first, gain_grad = norm_back(x_ref[...], gain_ref[...], acc_ref[...])
        gg_ref[...] = gain_grad
        store_halves(out_ref, r_ref[0], base_ref[...] + first)


def encoder_grad_kernel(r_ref, out_in, d_ref, w00, w10, w01, w11, out_ref, layer_ref, acc_ref):
    j = pl.program_id(0)
    part = dot_t(d_ref[0], by_columns(w00, w10, w01, w11))

    @pl.when(j == 0)
    def _():
        acc_ref[...] = part
        store_halves(layer_ref, r_ref[0], out_in[...])

    @pl.when(j == 1)
    def _():
        store_halves(out_ref, r_ref[0], acc_ref[...] + part)


SCALAR = pl.BlockSpec(memory_space=pltpu.SMEM)


def whole(shape):
    return pl.BlockSpec(shape, lambda *grid: (0,) * len(shape))


def square(row):
    return pl.BlockSpec((HALF, HALF), lambda *grid: (row, 0))


def moving(first):
    return pl.BlockSpec((HALF, HALF), lambda j: (first + j, 0))


def shaped(*shape, dtype=f32):
    return jax.ShapeDtypeStruct(shape, dtype)


def call(kernel, operands, in_specs, out_shape, out_specs, grid=(1,), scratch=(), flops=0):
    moved = sum(x.size * x.dtype.itemsize for x in operands)
    return pl.pallas_call(
        kernel,
        grid=grid,
        in_specs=in_specs,
        out_specs=out_specs,
        out_shape=out_shape,
        scratch_shapes=list(scratch),
        cost_estimate=cost(flops, moved),
        compiler_params=pltpu.CompilerParams(vmem_limit_bytes=56 << 20),
    )(*operands)


def added(a, b):
    return (a.astype(f32) + b.astype(f32)).astype(bf16)


def side_of(bit):
    return lax.bitwise_and(lax.div(lax.axis_index("dp"), jnp.int32(bit)), jnp.int32(1))


def chosen(side, low, high):
    return jnp.where(side == 0, low, high), jnp.where(side == 0, high, low)


QUARTER = HALF // 2


def over_dp(bit, x):
    count = lax.axis_size("dp")
    return lax.ppermute(x, "dp", [(i, i ^ bit) for i in range(count)])


def row_first(own, came):
    total = added(own, came)
    keep, send = pin(total[:, :HALF], total[:, HALF:])
    (came,) = yield (over_row(send),)
    total = added(keep, came)
    keep, send = chosen(side_of(1), total[:, :QUARTER], total[:, QUARTER:])
    (came,) = yield (over_dp(1, send),)
    yield added(keep, came)


def dp_first(own, came):
    total = added(own, came)
    total = total.reshape(total.shape[0], 2, 2, QUARTER, total.shape[2])
    keep, send = pin(*chosen(side_of(1), total[:, :, 0], total[:, :, 1]))
    (came,) = yield (over_dp(1, send),)
    total = added(keep, came)
    (came,) = yield (over_row(total[:, 1]),)
    yield added(total[:, 0], came)


def beyond(dp_count, block):
    undo = [1]
    bit = 2
    while bit < dp_count:
        rows = block.shape[1]
        if rows % 32 == 0:
            block, send = chosen(side_of(bit), block[:, : rows // 2], block[:, rows // 2 :])
            undo.append(bit)
        else:
            send = block
        (came,) = yield (over_dp(bit, send),)
        block = added(block, came)
        bit *= 2
    for bit in reversed(undo):
        (came,) = yield (over_dp(bit, block),)
        first, second = chosen(side_of(bit), block, came)
        block = jnp.concatenate([first, second], axis=1)
    yield block.astype(f32)


def small_sum(dp_count, small):
    (came,) = yield (over_col(small[:, 1]),)
    small = small[:, 0] + came
    (came,) = yield (over_row(small[1]),)
    small = small[0] + came
    bits = [1 << i for i in range(dp_count.bit_length() - 1)]
    for bit in bits[1:] + bits[:1]:
        (came,) = yield (over_dp(bit, small),)
        small = small + came
    yield small


def row_reduction(dp_count, own, came):
    a = row_first(own, came)
    came = yield next(a)
    came = yield a.send(came)
    yield from beyond(dp_count, a.send(came))


def whole_reduction(dp_count, left, right):
    a, b = row_first(*left), dp_first(*right)
    came = yield next(a) + next(b)
    came = yield a.send(came[:1]) + b.send(came[1:])
    block = jnp.concatenate([a.send(came[:1]), b.send(came[1:])], axis=0)
    yield from beyond(dp_count, block)


def local(
    layer_input,
    encoder_states,
    cotangent,
    buckets,
    gain_self,
    gain_cross,
    gain_ffn,
    self_query,
    self_key,
    self_value,
    self_out,
    cross_query,
    cross_key,
    cross_value,
    cross_out,
    ffn_gate,
    ffn_up,
    ffn_down,
    rel_table,
    dp_count,
):
    r = lax.axis_index("row")
    c = lax.axis_index("col")
    own_small = jnp.concatenate([gain_self, gain_cross, gain_ffn, rel_table.reshape(-1)])
    quarter = gain_self.shape[0]
    onehot = (buckets[:, None] == jnp.arange(NB, dtype=jnp.int32)[None, :]).astype(f32)
    placed = jnp.roll(onehot[::-1], LEN - BLK + 1, axis=0)
    tokens = layer_input.shape[0]
    row_index = jnp.reshape(r, (1,))
    both = range(2)
    tok = whole((tokens, D))
    tok_half = whole((tokens, HALF))
    vec = whole((1, D))
    tok_f32, tok_bf16 = shaped(tokens, D), shaped(tokens, D, dtype=bf16)
    half_bf16 = shaped(tokens, HALF, dtype=bf16)
    dense = 2 * tokens * D * HALF

    tokens = layer_input.shape[0]
    row_index = jnp.reshape(r, (1,))
    tok = whole((tokens, D))
    vec = whole((1, D))
    tok_f32, tok_bf16 = shaped(tokens, D), shaped(tokens, D, dtype=bf16)
    dense = 2 * tokens * D * D
    column = pl.BlockSpec((tokens, D), lambda j: (0, j))

    def gathered(own, arrived):
        return [own, arrived, over_col(own), over_col(arrived)]

    width = ffn_gate.shape[1]
    part = width // 2
    small_row = over_row(own_small)
    msg_self = stacked(self_query, self_key, self_value)
    msg_self, small_row, rest_weights = pin(
        msg_self,
        small_row,
        (self_out, cross_query, cross_key, cross_value, cross_out, ffn_down, ffn_gate, ffn_up),
    )
    got_self = over_row(msg_self)
    msg_mid = stacked(*rest_weights[:5])
    msg_down = rest_weights[5]
    msg_up = stacked(*rest_weights[6:])
    side = side_of(1)
    half_up = jnp.where(side == 0, msg_up[:HALF], msg_up[HALF:])
    small_row, msg_mid, msg_up, msg_down, half_up = pin(
        small_row, msg_mid, msg_up, msg_down, half_up
    )
    by_row = jnp.stack([own_small, small_row], axis=0)
    by_both = jnp.stack([by_row, over_col(by_row)], axis=1)
    by_col = local_order(by_both, c, 1)
    gains = [by_col[:, :, i * quarter : (i + 1) * quarter].reshape(1, D) for i in range(3)]
    tables = local_order(by_both, r, 0)[:, :, 3 * quarter :].transpose(1, 0, 2)
    bias_rows = lax.dot_general(
        tables.reshape(12, NB), placed, (((1,), (1,)), ((), ())), precision=lax.Precision.HIGHEST
    ).reshape(PAIRS, 2, LEN)

    w_self = gathered(msg_self, got_self)
    msg_mid, got_self, bias_rows = pin(msg_mid, got_self, bias_rows)
    got_mid = over_row(msg_mid)
    so, cqw, ckw, cvw, cow = range(5)
    normed_one, x, qkv = call(
        pre_self_kernel,
        [row_index, layer_input, gains[0]] + w_self,
        [SCALAR, tok, vec] + [moving(0)] * 4,
        [tok_bf16, tok_f32, shaped(tokens, 3 * D, dtype=bf16)],
        [tok, tok, column],
        grid=(3,),
        flops=3 * dense,
    )
    self_att, self_probs = attention_fwd(qkv, 0, qkv, PAIRS, qkv, 2 * PAIRS, bias_rows)
    self_att, got_mid, half_up, msg_down = pin(self_att, got_mid, half_up, msg_down)
    w_mid = gathered(msg_mid, got_mid)
    half_up = over_row(half_up)
    encoder, kv = call(
        encoder_kernel,
        [row_index, encoder_states] + w_mid,
        [SCALAR, tok] + [moving(ckw)] * 4,
        [tok_bf16, shaped(tokens, 2 * D, dtype=bf16)],
        [tok, column],
        grid=(2,),
        flops=2 * dense,
    )
    middle, normed_two, cq = call(
        join_kernel,
        [x, self_att] + w_mid + [gains[1]] + w_mid,
        [tok, tok] + [square(so)] * 4 + [vec] + [square(cqw)] * 4,
        [tok_f32, tok_bf16, tok_bf16],
        [tok, tok, tok],
        flops=2 * dense,
    )
    cq, kv, msg_down, half_up = pin(cq, kv, msg_down, half_up)
    got_down = over_row(msg_down)
    other_up = over_dp(1, half_up)
    cross_att, cross_probs = attention_fwd(cq, 0, kv, 0, kv, PAIRS, None)
    cross_att, half_up, other_up = pin(cross_att, half_up, other_up)
    got_up = jnp.concatenate(chosen(side, half_up, other_up), axis=0)
    after, normed_three = call(
        join_kernel,
        [middle, cross_att] + w_mid + [gains[2]],
        [tok, tok] + [square(cow)] * 4 + [vec],
        [tok_f32, tok_bf16],
        [tok, tok],
        flops=dense,
    )

    w_up = gathered(msg_up, got_up)
    normed_three, got_down = pin(normed_three, got_down)
    w_down = gathered(msg_down, got_down)
    tile = 512
    per = part // tile
    layer_local, ng, out_low = after, after, cotangent
    ffn_grads = [None, None]
    for h in (1, 0):
        up, down = w_up[2 * h : 2 * h + 2], w_down[2 * h : 2 * h + 2]
        layer_local, ng, out_low, ffn_grads[h] = call(
            functools.partial(ffn_kernel, h == 1),
            [row_index, normed_three, out_low, layer_local, ng] + up + up + down,
            [SCALAR]
            + [tok] * 4
            + [pl.BlockSpec((HALF, tile), lambda t: (0, t))] * 2
            + [pl.BlockSpec((HALF, tile), lambda t: (1, t))] * 2
            + [pl.BlockSpec((tile, HALF), lambda t: (t, 0))] * 2,
            [tok_f32, tok_f32, tok_bf16, shaped(3, 2, D, part, dtype=bf16)],
            [tok] * 3 + [pl.BlockSpec((3, 1, D, tile), lambda t: (0, t // per, 0, t % per))],
            grid=(width // tile,),
            scratch=[pltpu.VMEM((D, tokens), bf16)] * 2,
            flops=9 * 2 * tokens * D * width,
        )
        if h == 1:
            came = over_col(ffn_grads[1])
    out_low, ffn_grads[0], came, ng = pin(out_low, ffn_grads[0], came, ng)
    ffn_a = row_first(ffn_grads[0][:, 0], came[:, 0])
    ffn_b = dp_first(ffn_grads[0][:, 1], came[:, 1])
    came_a, came_b = next(ffn_a), next(ffn_b)
    after_grad, after_low, cross_mixed, gain_ffn_grad = call(
        after_ffn_kernel,
        [row_index, after, cotangent, ng, gains[2]] + w_mid,
        [SCALAR, tok, tok, tok, vec] + [square(cow)] * 4,
        [tok_f32, tok_bf16, tok_bf16, shaped(1, D)],
        [tok, tok, tok, vec],
        flops=dense,
    )
    (cross_back,) = attention_bwd(cq, 0, kv, 0, kv, PAIRS, cross_mixed, cross_probs, False)
    cross_back, came_a, came_b = pin(cross_back, came_a, came_b)
    came_a, came_b = ffn_a.send(came_a), ffn_b.send(came_b)
    middle_grad, middle_low, self_mixed, gain_cross_grad = call(
        after_cross_kernel,
        [middle, after_grad, cross_back] + w_mid + [gains[1]] + w_mid,
        [tok, tok, pl.BlockSpec((1, tokens, D), lambda j: (0, 0, 0))]
        + [square(cqw)] * 4
        + [vec]
        + [square(so)] * 4,
        [tok_f32, tok_bf16, tok_bf16, shaped(1, D)],
        [tok, tok, tok, vec],
        flops=2 * dense,
    )
    pieces = shaped(5, D, HALF, dtype=bf16)
    cross_own, cross_other = call(
        cross_grads_kernel,
        [encoder, normed_two, after_low, middle_low, cross_back, cross_att, self_att],
        [tok] * 4 + [whole((3, tokens, D))] + [tok] * 2,
        [pieces, pieces],
        [whole((5, D, HALF))] * 2,
        flops=5 * dense,
    )
    self_mixed, cross_other, came_a, came_b = pin(self_mixed, cross_other, came_a, came_b)
    ffn = beyond(dp_count, jnp.concatenate([ffn_a.send(came_a), ffn_b.send(came_b)], axis=0))
    ffn_came = next(ffn)
    cross_came = over_col(cross_other)

    self_back, shifts, self_grads = [None, None], [None, None], [None, None]

    def self_half(h):
        back, shift = attention_bwd(
            qkv, 0, qkv, PAIRS, qkv, 2 * PAIRS, self_mixed, self_probs, True, h * PAIRS // 2, PAIRS // 2
        )
        return back, shift

    def self_half_grads(back):
        return call(
            self_grads_kernel,
            [normed_one, back],
            [tok, pl.BlockSpec((1, tokens, HALF), lambda j: (j, 0, 0))],
            shaped(3, D, HALF, dtype=bf16),
            pl.BlockSpec((1, D, HALF), lambda j: (j, 0, 0)),
            grid=(3,),
            scratch=[pltpu.VMEM((D, tokens), bf16)],
            flops=3 * dense // 2,
        )

    self_back[1], shifts[1] = self_half(1)
    self_back[1], self_mixed, cross_came, ffn_came = pin(
        self_back[1], self_mixed, cross_came, ffn_came
    )
    cross = whole_reduction(
        dp_count, (cross_own[:3], cross_came[:3]), (cross_own[3:], cross_came[3:])
    )
    cross_came = next(cross)
    ffn_came = ffn.send(ffn_came)
    self_grads[1] = self_half_grads(self_back[1])
    self_mixed, self_grads[1] = pin(self_mixed, self_grads[1])
    self_came = over_col(self_grads[1])
    self_back[0], shifts[0] = self_half(0)
    self_back[0], ffn_came = pin(self_back[0], ffn_came)
    ffn_came = ffn.send(ffn_came)
    self_grads[0] = self_half_grads(self_back[0])
    self_grads[0], self_came, cross_came, middle_grad, layer_local = pin(
        self_grads[0], self_came, cross_came, middle_grad, layer_local
    )
    own = row_reduction(dp_count, self_grads[0], self_came)
    self_came = next(own)
    cross_came = cross.send(cross_came)
    encoder_grad, layer_output = call(
        encoder_grad_kernel,
        [row_index, layer_local, cross_back] + w_mid,
        [SCALAR, tok, pl.BlockSpec((1, tokens, D), lambda j: (1 + j, 0, 0))] + [moving(ckw)] * 4,
        [tok_f32, tok_f32],
        [tok, tok],
        grid=(2,),
        scratch=[pltpu.VMEM((tokens, D), f32)],
        flops=2 * dense,
    )
    cross_came, ffn_came, middle_grad, layer_output = pin(
        cross_came, ffn_came, middle_grad, layer_output
    )
    cross_came = cross.send(cross_came)
    ffn_came = ffn.send(ffn_came)
    one = pl.BlockSpec((1, tokens, HALF), lambda j: (j, 0, 0))
    input_grad, gain_self_grad = call(
        input_grad_kernel,
        [row_index, x, middle_grad, gains[0], self_back[0], self_back[1]] + w_self,
        [SCALAR, tok, tok, vec, one, one] + [moving(0)] * 4,
        [tok_f32, shaped(1, D)],
        [tok, vec],
        grid=(3,),
        scratch=[pltpu.VMEM((tokens, D), f32)],
        flops=3 * dense,
    )
    shift_sums = jnp.concatenate(
        [jnp.sum(part_sums.reshape(-1, PAIRS, LEN), axis=0) for part_sums in shifts], axis=0
    )
    table_local = jnp.dot(
        shift_sums, placed, precision=lax.Precision.HIGHEST
    ).reshape(2, 2, 3 * NB)
    table_local = local_order(table_local, r, 1).transpose(1, 0, 2)
    gains_local = jnp.stack([gain_self_grad, gain_cross_grad, gain_ffn_grad], axis=0)
    gains_local = local_order(gains_local.reshape(3, 2, 2, quarter), c, 2)
    gains_local = gains_local.transpose(1, 2, 0, 3).reshape(2, 2, 3 * quarter)
    small = jnp.concatenate([gains_local, table_local], axis=2)
    groups = [own, cross, ffn, small_sum(dp_count, small)]
    under_way = [self_came, cross_came, ffn_came, None]
    small, under_way[0], under_way[1], under_way[2] = pin(small, *under_way[:3])
    sums = [None] * 4
    while any(total is None for total in sums):
        live = [i for i in range(4) if sums[i] is None]
        if len(live) > 1 and under_way[2] is not None and under_way[2][0].shape[1] == QUARTER:
            live = [i for i in live if i != 2]
        arrived = _pinned([under_way[i] for i in live])
        for i, came in zip(live, arrived):
            started = next(groups[i]) if came is None else groups[i].send(came)
            if isinstance(started, tuple):
                under_way[i] = started
            else:
                sums[i] = started
    self_sum, cross_sum, ffn_sum, small = sums
    gains_own = small[: 3 * quarter].reshape(3, quarter)
    table_own = small[3 * quarter :].reshape(1, 1, 3, NB)

    ffn_sum = ffn_sum.reshape(2, 3, HALF, part)
    gate_sum, up_sum = (
        jnp.concatenate([ffn_sum[0, k], ffn_sum[1, k]], axis=1) for k in range(2)
    )
    down_sum = jnp.concatenate([ffn_sum[0, 2].T, ffn_sum[1, 2].T], axis=0)
    return (
        layer_output,
        input_grad,
        encoder_grad,
        gains_own[0],
        gains_own[1],
        gains_own[2],
        self_sum[0],
        self_sum[1],
        self_sum[2],
        cross_sum[4].T,
        cross_sum[2],
        cross_sum[0],
        cross_sum[1],
        cross_sum[3].T,
        gate_sum,
        up_sum,
        down_sum,
        table_own,
    )


def solution(mesh):
    tokens = P(("dp", "row", "col"), None)
    gain = P(("row", "col"))
    columns = P("row", "col")
    rows = P("col", "row")
    table = P("col", "row", None, None)
    weights = (columns,) * 3 + (rows,) + (columns,) * 3 + (rows,) + (columns,) * 2 + (rows,)
    in_specs = (tokens,) * 3 + (P(),) + (gain,) * 3 + weights + (table,)
    out_specs = (tokens,) * 3 + (gain,) * 3 + weights + (table,)
    body = functools.partial(local, dp_count=mesh.shape["dp"])
    return jax.shard_map(
        body, mesh=mesh, in_specs=in_specs, out_specs=out_specs, check_vma=False
    )
```
